768 devices in a mesh: batch: 192 (over x, y, z_lo), seq: 4 (over z_hi, core).
Axes of the slice: x: 4, y: 8, z: 12 (z_hi: 2, z_lo: 6; z = z_hi * 6 + z_lo), core: 2. Of those that a mesh axis runs over, the one named last changes fastest.
Arguments:
- track_input: bfloat16 [294912, 768], P(('batch', 'seq')), parts along dimension 0, may hold values from -6 to 6
- conv_gain: float32 [4, 768], replicated, may hold values from 0.1 to 1.9
- conv_kernel: float32 [4, 5, 768], replicated, may hold values from -3 to 3
- dilation: int32 [4], replicated, may hold values from 1 to 8, as said below
- attn_gain: float32 [768], replicated, may hold values from 0.1 to 1.9
- w_qkv: bfloat16 [768, 2304], replicated, as said below
- w_out: bfloat16 [768, 768], replicated, may hold values from -1.75 to 1.75
- w_pair_a: bfloat16 [768, 512], replicated, may hold values from -0.21875 to 0.21875
- w_pair_b: bfloat16 [768, 512], replicated, may hold values from -0.21875 to 0.21875
Outputs:
- track_out: bfloat16 [294912, 768], P(('batch', 'seq')), parts along dimension 0
- pair_map: bfloat16 [12288, 96, 96], P('batch', 'seq'), parts along dimension 0
The draws below stay inside these ranges and needn't reach their ends.
There are 192 independent parts, one for each index of `batch`. The reference program is written for one: setup_inputs(seed, part) draws one part's arguments, and reference() takes and returns one part's arrays. A program takes and returns all parts, laid end to end along the dimension named above; an argument that names none is the same for every part. Nothing has to cross between parts.
Inputs may be any that keep to these rules, and one draw needn't show every extreme that they name: Every dilation lies in 1 to 8; exactly one layer has dilation 8, the others less. `w_qkv`: a projection matrix with entries of order 768^-0.5 or larger.
All inputs are finite; a program needn't handle non-finite values.
Results may differ from the reference program's by a relative error of at most 0.019.
The reference program's roundings to bfloat16 on the way count: a program that leaves them out, or rounds other values in their place, can miss the bound.
Values may be sent and summed in bfloat16 or wider, within the bound.
A program may use at most 64 MiB of HBM per device.

```python
import math
import jax
import jax.numpy as jnp
from jax import lax

C = 768
HEADS = 8
DH = 96
KSIZE = 5
DMAX = 8
LAYERS = 4
POOL = 16
PCH = 64
R = 8
NTOT = 1536
NPAIR = 96


def draw_dilation(key, part):
    rates = jax.random.randint(key, (LAYERS,), 1, DMAX)
    chosen = jax.random.randint(jax.random.fold_in(key, 7), (), 0, LAYERS)
    rates = jnp.where(jnp.arange(LAYERS) == chosen, DMAX, rates)
    return rates.astype(jnp.int32)


def draw_w_qkv(key, part):
    matrix = jax.random.normal(key, (C, 3 * C), jnp.float32) * C ** (-0.5)
    return matrix.astype(jnp.bfloat16)


def shard_levels(key, dims, shards, least, top_value):
    level = 1.0
    for dim, shards_of in shards:
        steps = jax.random.uniform(jax.random.fold_in(jax.random.fold_in(key, 6), dim), (shards_of,), jnp.float32, least / len(shards), top_value / len(shards))
        level = level * jnp.repeat(jnp.exp(steps), dims[dim] // shards_of).reshape((-1,) + (1,) * (len(dims) - 1 - dim))
    return level


def normal_values(stream_key, shape, width, most, shards=(), kind=jnp.bfloat16):
    entries = width * jax.random.normal(stream_key, shape, jnp.float32)
    if shards:
        entries = entries * shard_levels(stream_key, shape, shards, -0.22, 0.18)
    return jnp.clip(entries, -most, most).astype(kind)


def setup_inputs(seed: int = 0, part: int = 0) -> dict:
    key_of = jax.random.split(jax.random.key(seed), 10)
    own_keys = jax.random.split(jax.random.fold_in(key_of[9], part), 10)
    track_input = normal_values(own_keys[0], (NTOT, C), 1.0, 6.0, ((0, 4),))
    conv_gain = jnp.clip(1.0 + 0.18 * jax.random.normal(key_of[1], (LAYERS, C), jnp.float32), 0.1, 1.9)
    conv_kernel = normal_values(key_of[2], (LAYERS, KSIZE, C), 0.5, 3.0, (), jnp.float32)
    dilation = draw_dilation(jax.random.fold_in(key_of[9], 71), part)
    attn_gain = jnp.clip(1.0 + 0.18 * jax.random.normal(key_of[4], (C,), jnp.float32), 0.1, 1.9)
    w_qkv = draw_w_qkv(jax.random.fold_in(key_of[9], 71), part)
    w_out = normal_values(key_of[6], (C, C), (max(C // 64, 1)) ** -0.5, 1.75)
    w_pair_a = normal_values(key_of[7], (C, R * PCH), C ** -0.5, 0.21875)
    w_pair_b = normal_values(key_of[8], (C, R * PCH), C ** -0.5, 0.21875)
    return {"track_input": track_input, "conv_gain": conv_gain, "conv_kernel": conv_kernel, "dilation": dilation, "attn_gain": attn_gain, "w_qkv": w_qkv, "w_out": w_out, "w_pair_a": w_pair_a, "w_pair_b": w_pair_b}


def rms_norm(values, gain):
    return values * lax.rsqrt(lax.optimization_barrier(jnp.mean(values * values, axis=-1, keepdims=True)) + 1e-06) * gain

def dilated_conv(padded, norm_gain, kernel, dilation_rate, out_len):
    rim_width = KSIZE // 2 * DMAX
    normed = rms_norm(padded, norm_gain)
    total = jnp.zeros((out_len, padded.shape[1]), jnp.float32)
    for tap_index in range(KSIZE):
        start = (rim_width + (tap_index - KSIZE // 2) * dilation_rate).astype(jnp.int32)
        total = total + kernel[tap_index] * lax.dynamic_slice_in_dim(normed, start, out_len, 0)
    return padded[rim_width:rim_width + out_len] + jax.nn.gelu(total)

def attend_head(operands):
    query_head, key_head, value_head = operands
    scores = jnp.dot(query_head, key_head.T, preferred_element_type=jnp.float32) / math.sqrt(DH)
    weights = jax.nn.softmax(scores, axis=-1).astype(jnp.bfloat16)
    return jnp.dot(weights, value_head, preferred_element_type=jnp.float32)

def reference(track_input, conv_gain, conv_kernel, dilation, attn_gain, w_qkv, w_out, w_pair_a, w_pair_b):
    rim_width = KSIZE // 2 * DMAX
    layer_state = track_input.astype(jnp.float32)
    for layer in range(LAYERS):
        padded = jnp.pad(layer_state, ((rim_width, rim_width), (0, 0)))
        layer_state = dilated_conv(padded, conv_gain[layer], conv_kernel[layer], dilation[layer], NTOT)
    normed = rms_norm(layer_state, attn_gain).astype(jnp.bfloat16)
    projected = jnp.dot(normed, w_qkv, preferred_element_type=jnp.float32).astype(jnp.bfloat16)

    def split_heads(block):
        return block.reshape(NTOT, HEADS, DH).transpose(1, 0, 2)
    head_out = lax.map(attend_head, (split_heads(projected[:, :C]), split_heads(projected[:, C:2 * C]), split_heads(projected[:, 2 * C:])))
    mixed = head_out.transpose(1, 0, 2).reshape(NTOT, C).astype(jnp.bfloat16)
    output = layer_state + jnp.dot(mixed, w_out, preferred_element_type=jnp.float32)
    pooled = rms_norm(output.reshape(NPAIR, POOL, C).mean(axis=1), 1.0).astype(jnp.bfloat16)
    left_side = jnp.dot(pooled, w_pair_a, preferred_element_type=jnp.float32).astype(jnp.bfloat16).reshape(NPAIR, R, PCH)
    right_side = jnp.dot(pooled, w_pair_b, preferred_element_type=jnp.float32).astype(jnp.bfloat16).reshape(NPAIR, R, PCH)
    pair_map = jnp.einsum('irc,jrc->cij', left_side.astype(jnp.float32), right_side.astype(jnp.float32), precision=lax.Precision.HIGHEST) / math.sqrt(R)
    return (output.astype(jnp.bfloat16), pair_map.astype(jnp.bfloat16))
```

```python
import math

import jax
import jax.numpy as jnp
from jax import lax
from jax.experimental import pallas as pl
from jax.experimental.pallas import tpu as pltpu
from jax.sharding import PartitionSpec as P

C = 768
HEADS = 8
KSIZE = 5
LAYERS = 4
POOL = 16
PCH = 64
R = 8
ROWS = 384
GROUP = 4
LANES = 128
CT = C // LANES
REACH = 16
EDGE = LAYERS * REACH
SEG = ROWS // 8
CHUNK = 128
PAIRS = HEADS // 2
WIN = 256
BF = jnp.bfloat16
F32 = jnp.float32
MESH = pl.DeviceIdType.MESH
LOG2E = math.log2(math.e)


def gelu(v):
    u = v * (math.sqrt(2 / math.pi) + math.sqrt(2 / math.pi) * 0.044715 * (v * v))
    half = 0.5 * v
    return half + half * jnp.tanh(u)


def conv_stack(nat, seg, hbuf, taps_ref, dil_ref, low, high):
    def load(q, _):
        for c in range(CT):
            seg[c, q] = nat[c, pl.ds(q, 8, stride=SEG), :]
        return 0

    lax.fori_loop(0, SEG, load, 0)

    def layer(l, _):
        d = dil_ref[l]

        def norm(k, _):
            q = pl.multiple_of(k * 8, 8)
            rows = [seg[c, pl.ds(q, 8)] for c in range(CT)]
            total = rows[0] * rows[0]
            for c in range(1, CT):
                total = total + rows[c] * rows[c]
            mean = jnp.sum(total, axis=-1, keepdims=True) * (1.0 / C)
            place = (
                lax.broadcasted_iota(jnp.int32, (8, 8, 1), 1) * SEG
                + lax.broadcasted_iota(jnp.int32, (8, 8, 1), 0)
                + q
            )
            scale = jnp.where((place >= low) & (place < high), lax.rsqrt(mean + 1e-06), 0.0)
            for c in range(CT):
                hbuf[c, pl.ds(q + REACH, 8)] = rows[c] * scale
            return 0

        lax.fori_loop(0, SEG // 8, norm, 0)
        for c in range(CT):
            hbuf[c, 0:REACH] = pltpu.roll(hbuf[c, SEG : SEG + REACH], 1, 1)
            hbuf[c, SEG + REACH : SEG + 2 * REACH] = pltpu.roll(
                hbuf[c, REACH : 2 * REACH], 7, 1
            )
        for c in range(CT):
            cols = slice(c * LANES, (c + 1) * LANES)
            taps = [
                jnp.broadcast_to(taps_ref[l, t : t + 1, cols], (8, LANES))[None]
                for t in range(KSIZE)
            ]

            def conv(k, _):
                q = pl.multiple_of(k * 8, 8)
                total = taps[0] * hbuf[c, pl.ds(q + REACH - 2 * d, 8)]
                for t in range(1, KSIZE):
                    total = total + taps[t] * hbuf[c, pl.ds(q + REACH + (t - 2) * d, 8)]
                seg[c, pl.ds(q, 8)] = seg[c, pl.ds(q, 8)] + gelu(total)
                return 0

            lax.fori_loop(0, SEG // 8, conv, 0)
        return 0

    lax.fori_loop(0, LAYERS, layer, 0)

    def store(q, _):
        for c in range(CT):
            nat[c, pl.ds(q, 8, stride=SEG), :] = seg[c, q]
        return 0

    lax.fori_loop(0, SEG, store, 0)


def kernel(
    x_ref, gain_ref, taps_ref, dil_ref, again_ref, wqkv_hbm, wout_hbm, wa_hbm, wb_hbm,
    track_ref, pair_ref,
    wqkv, wout, wa, wb, scaled, nat, seg, hbuf, state, halo, near, far, keys, values, q2,
    top, mass, acc, mixed, rights, wsem, send, recv,
):
    block = lax.axis_index("seq")
    core = lax.rem(block, 2)
    sibling = block + 1 - 2 * core
    partner = lax.rem(block + 2, GROUP)
    cross = GROUP - 1 - block

    def remote(src, dst, index, target):
        return pltpu.make_async_remote_copy(
            src_ref=src, dst_ref=dst, send_sem=send.at[index], recv_sem=recv.at[index],
            device_id={"seq": target}, device_id_type=MESH,
        )

    weights = [
        pltpu.make_async_copy(src, dst, wsem.at[i])
        for i, (src, dst) in enumerate(
            ((wqkv_hbm, wqkv), (wout_hbm, wout), (wa_hbm, wa), (wb_hbm, wb))
        )
    ]
    for copy in weights:
        copy.start()
    barrier = pltpu.get_barrier_semaphore()
    for target in (sibling, partner, cross):
        pl.semaphore_signal(barrier, inc=1, device_id={"seq": target}, device_id_type=MESH)

    for l in range(LAYERS):
        scaled[l] = taps_ref[l] * gain_ref[l : l + 1]
    for c in range(CT):
        nat[c] = x_ref[:, c * LANES : (c + 1) * LANES].astype(F32)
    conv_stack(nat, seg, hbuf, scaled, dil_ref, 0, ROWS)

    def finish(source, target, count):
        rows = [nat[c, source : source + count] for c in range(CT)]
        total = rows[0] * rows[0]
        for c in range(1, CT):
            total = total + rows[c] * rows[c]
        scale = lax.rsqrt(jnp.sum(total, axis=-1, keepdims=True) * (1.0 / C) + 1e-06)
        for c in range(CT):
            cols = slice(c * LANES, (c + 1) * LANES)
            state[c, target : target + count] = rows[c]
            near[0, target : target + count, cols] = (
                rows[c] * scale * again_ref[:, cols]
            ).astype(BF)

    for start in range(EDGE, ROWS - EDGE, 64):
        finish(start, start, 64)
    pl.semaphore_wait(barrier, 3)

    to_left = remote(x_ref.at[pl.ds(0, EDGE)], halo.at[1], 0, lax.rem(block + GROUP - 1, GROUP))
    to_right = remote(
        x_ref.at[pl.ds(ROWS - EDGE, EDGE)], halo.at[0], 1, lax.rem(block + 1, GROUP)
    )
    has_left, has_right = block > 0, block < GROUP - 1

    @pl.when(has_left)
    def _():
        to_left.start()

    @pl.when(has_right)
    def _():
        to_right.start()

    inner = [
        remote(near.at[0, pl.ds(EDGE + i * CHUNK, CHUNK)], far.at[2 * i], 2 + i, partner)
        for i in range(2)
    ]
    inner_near = remote(
        near.at[0, pl.ds(EDGE, 2 * CHUNK)], near.at[1, pl.ds(EDGE, 2 * CHUNK)], 6, sibling
    )
    inner_near.start()
    for copy in inner:
        copy.start()

    @pl.when(has_left)
    def _():
        to_right.wait_recv()

    @pl.when(jnp.logical_not(has_left))
    def _():
        halo[0] = jnp.zeros((EDGE, C), BF)

    @pl.when(has_right)
    def _():
        to_left.wait_recv()

    @pl.when(jnp.logical_not(has_right))
    def _():
        halo[1] = jnp.zeros((EDGE, C), BF)

    for c in range(CT):
        cols = slice(c * LANES, (c + 1) * LANES)
        nat[c, 0:EDGE] = halo[0, :, cols].astype(F32)
        nat[c, EDGE : 3 * EDGE] = x_ref[0 : 2 * EDGE, cols].astype(F32)
        nat[c, 3 * EDGE : 5 * EDGE] = x_ref[ROWS - 2 * EDGE :, cols].astype(F32)
        nat[c, 5 * EDGE :] = halo[1, :, cols].astype(F32)
    conv_stack(
        nat, seg, hbuf, scaled, dil_ref,
        jnp.where(has_left, 0, EDGE), jnp.where(has_right, ROWS, ROWS - EDGE),
    )
    finish(EDGE, 0, EDGE)
    finish(ROWS - 2 * EDGE, ROWS - EDGE, EDGE)
    outer = []
    for i, start in enumerate((0, ROWS - EDGE)):
        rows = pl.ds(start, EDGE)
        outer.append(remote(near.at[0, rows], far.at[4, pl.ds(i * EDGE, EDGE)], 4 + i, partner))
        outer.append(remote(near.at[0, rows], near.at[1, rows], 7 + i, sibling))
    for copy in outer:
        copy.start()

    weights[0].wait()

    lane = lax.broadcasted_iota(jnp.int32, (1, WIN), 1)

    def project(source, column):
        return jnp.dot(
            source, wqkv[:, pl.ds(pl.multiple_of(column, LANES), WIN)],
            preferred_element_type=F32,
        ).astype(BF)

    def window(p):
        return (p // 2) * (3 * LANES) + lax.rem(p, 2) * LANES

    def queries(p, _):
        rows = project(near[0], window(p))
        first = lax.rem(p, 2) * 64
        for i in range(2):
            mine = (lane >= first + 96 * i) & (lane < first + 96 * (i + 1))
            q2[p, i * ROWS : (i + 1) * ROWS] = jnp.where(mine, rows, jnp.zeros_like(rows))
        return 0

    lax.fori_loop(0, PAIRS, queries, 0)

    def keys_values(load, place, count):
        def tile(t, _):
            cols = pl.ds(pl.multiple_of(t * WIN, WIN), WIN)
            source = load()
            keys[place : place + count, cols] = project(source, C + t * WIN)
            values[place : place + count, cols] = project(source, 2 * C + t * WIN)
            return 0

        lax.fori_loop(0, C // WIN, tile, 0)

    TILE = 256
    SCALE = LOG2E / math.sqrt(C // HEADS)

    def attend(place, count, fresh):
        def pair(p, _):
            cols = pl.ds(pl.multiple_of(window(p), LANES), WIN)

            def tile(t, _):
                rows = pl.ds(pl.multiple_of(t * TILE, TILE), TILE)
                scores = lax.dot_general(
                    q2[p, rows], keys[place : place + count, cols],
                    (((1,), (1,)), ((), ())), preferred_element_type=F32,
                )
                peak = jnp.max(scores, axis=-1, keepdims=True)
                if not fresh:
                    old = top[p, rows]
                    peak = jnp.maximum(peak, old)
                probs = jnp.exp2((scores - peak) * SCALE)
                part = jnp.sum(probs, axis=-1, keepdims=True)
                out = jnp.dot(
                    probs.astype(BF), values[place : place + count, cols],
                    preferred_element_type=F32,
                )
                if fresh:
                    mass[p, rows] = part
                    acc[p, rows] = out
                else:
                    rescale = jnp.exp2((old - peak) * SCALE)
                    mass[p, rows] = mass[p, rows] * rescale + part
                    acc[p, rows] = acc[p, rows] * rescale + out
                top[p, rows] = peak
                return 0

            lax.fori_loop(0, 2 * ROWS // TILE, tile, 0)
            return 0

        lax.fori_loop(0, PAIRS, pair, 0)

    keys_values(lambda: near[0], 0, ROWS)
    inner_near.wait_recv()
    outer[1].wait_recv()
    outer[3].wait_recv()
    keys_values(lambda: near[1], ROWS, ROWS)
    attend(0, 2 * ROWS, True)

    passes = []
    for i in range(3):
        for copy in ([inner[i]] if i < 2 else [outer[0], outer[2]]):
            copy.wait_recv()
        onward = remote(far.at[2 * i], far.at[2 * i + 1], 9 + i, sibling)
        onward.start()
        passes.append(onward)
        onward.wait_recv()
        place = 2 * ROWS + 2 * CHUNK * i
        keys_values(
            lambda i=i: far[2 * i : 2 * i + 2].reshape(2 * CHUNK, C), place, 2 * CHUNK
        )
        attend(place, 2 * CHUNK, False)

    for g in range(2):
        parts = []
        for j in range(2):
            p = 2 * g + j
            both = acc[p] / mass[p]
            first = j * 64
            one = (lane >= first) & (lane < first + 96)
            two = (lane >= first + 96) & (lane < first + 192)
            parts.append(
                jnp.where(one, both[:ROWS], jnp.where(two, both[ROWS:], 0.0))
            )
        base = g * 3 * LANES
        mixed[:, base : base + LANES] = parts[0][:, :LANES].astype(BF)
        mixed[:, base + LANES : base + 2 * LANES] = (
            parts[0][:, LANES:] + parts[1][:, :LANES]
        ).astype(BF)
        mixed[:, base + 2 * LANES : base + 3 * LANES] = parts[1][:, LANES:].astype(BF)

    weights[1].wait()
    squares = jnp.zeros((ROWS // POOL, LANES), F32)
    pools = []
    for t in range(C // WIN):
        product = jnp.dot(
            mixed[...], wout[:, t * WIN : (t + 1) * WIN], preferred_element_type=F32
        )
        for j in range(WIN // LANES):
            c = t * (WIN // LANES) + j
            result = state[c] + product[:, j * LANES : (j + 1) * LANES]
            track_ref[:, c * LANES : (c + 1) * LANES] = result.astype(BF)
            pool = jnp.sum(result.reshape(ROWS // POOL, POOL, LANES), axis=1) * (1.0 / POOL)
            squares = squares + pool * pool
            pools.append(pool)
    scale = lax.rsqrt(jnp.sum(squares, axis=-1, keepdims=True) * (1.0 / C) + 1e-06)
    pooled = jnp.concatenate([pool * scale for pool in pools], axis=1).astype(BF)
    weights[3].wait()
    right = jnp.dot(pooled, wb[...], preferred_element_type=F32).astype(BF)
    rights[pl.ds(block, 1)] = right[None]
    shares = [
        remote(rights.at[block], rights.at[block], 12 + i, target)
        for i, target in enumerate((sibling, partner, cross))
    ]
    for copy in shares[::-1]:
        copy.start()
    weights[2].wait()
    left = jnp.dot(pooled, wa[...], preferred_element_type=F32).astype(BF).astype(F32)
    channel = lax.rem(lax.broadcasted_iota(jnp.int32, (PCH, 1, R * PCH), 2), PCH)
    wanted = lax.broadcasted_iota(jnp.int32, (PCH, 1, R * PCH), 0)
    spread = jnp.where(channel == wanted, left[None], 0.0)
    spread = spread.reshape(PCH * (ROWS // POOL), R * PCH).astype(BF)
    for copy in shares:
        copy.wait_recv()
    every = jnp.concatenate([rights[i].astype(F32) for i in range(GROUP)], axis=0).astype(BF)
    product = lax.dot_general(
        spread, every, (((1,), (1,)), ((), ())), preferred_element_type=F32
    )
    pair_ref[...] = (
        (product * (1.0 / math.sqrt(R))).reshape(PCH, ROWS // POOL, GROUP * ROWS // POOL)
    ).astype(BF)

    @pl.when(has_left)
    def _():
        to_left.wait_send()

    @pl.when(has_right)
    def _():
        to_right.wait_send()

    for copy in inner + [inner_near] + outer + passes + shares:
        copy.wait_send()


def body(x, conv_gain, conv_kernel, dilation, attn_gain, w_qkv, w_out, w_pair_a, w_pair_b):
    vmem = pl.BlockSpec(memory_space=pltpu.VMEM)
    hbm = pl.BlockSpec(memory_space=pl.ANY)
    return pl.pallas_call(
        kernel,
        out_shape=(
            jax.ShapeDtypeStruct((ROWS, C), BF),
            jax.ShapeDtypeStruct((PCH, ROWS // POOL, GROUP * ROWS // POOL), BF),
        ),
        in_specs=[vmem, vmem, vmem, pl.BlockSpec(memory_space=pltpu.SMEM), vmem, hbm, hbm, hbm, hbm],
        out_specs=(vmem, vmem),
        scratch_shapes=[
            pltpu.VMEM(w_qkv.shape, BF),
            pltpu.VMEM(w_out.shape, BF),
            pltpu.VMEM(w_pair_a.shape, BF),
            pltpu.VMEM(w_pair_b.shape, BF),
            pltpu.VMEM((LAYERS, KSIZE, C), F32),
            pltpu.VMEM((CT, ROWS, LANES), F32),
            pltpu.VMEM((CT, SEG, 8, LANES), F32),
            pltpu.VMEM((CT, SEG + 2 * REACH, 8, LANES), F32),
            pltpu.VMEM((CT, ROWS, LANES), F32),
            pltpu.VMEM((2, EDGE, C), BF),
            pltpu.VMEM((2, ROWS, C), BF),
            pltpu.VMEM((6, CHUNK, C), BF),
            pltpu.VMEM((GROUP * ROWS, C), BF),
            pltpu.VMEM((GROUP * ROWS, C), BF),
            pltpu.VMEM((PAIRS, 2 * ROWS, WIN), BF),
            pltpu.VMEM((PAIRS, 2 * ROWS, 1), F32),
            pltpu.VMEM((PAIRS, 2 * ROWS, 1), F32),
            pltpu.VMEM((PAIRS, 2 * ROWS, WIN), F32),
            pltpu.VMEM((ROWS, C), BF),
            pltpu.VMEM((GROUP, ROWS // POOL, R * PCH), BF),
            pltpu.SemaphoreType.DMA((4,)),
            pltpu.SemaphoreType.DMA((15,)),
            pltpu.SemaphoreType.DMA((15,)),
        ],
        compiler_params=pltpu.CompilerParams(
            collective_id=0, has_side_effects=True, vmem_limit_bytes=60 * 1024 * 1024
        ),
    )(x, conv_gain, conv_kernel, dilation, attn_gain.reshape(1, C), w_qkv, w_out, w_pair_a, w_pair_b)


def solution(mesh):
    placed = (P(("batch", "seq"), None), P(), P(), P(), P(), P(), P(), P(), P())
    return jax.shard_map(
        body,
        mesh=mesh,
        in_specs=placed,
        out_specs=(P(("batch", "seq"), None), P("batch", "seq", None)),
        check_vma=False,
    )
```

```python
import math

import jax
import jax.numpy as jnp
from jax import lax
from jax.experimental import pallas as pl
from jax.experimental.pallas import tpu as pltpu
from jax.sharding import PartitionSpec as P

C = 768
HEADS = 8
KSIZE = 5
LAYERS = 4
POOL = 16
PCH = 64
R = 8
ROWS = 384
GROUP = 4
LANES = 128
CT = C // LANES
REACH = 16
EDGE = LAYERS * REACH
SEG = ROWS // 8
STEP = 8
CHUNK = 128
PAIRS = HEADS // 2
WIN = 256
BF = jnp.bfloat16
F32 = jnp.float32
MESH = pl.DeviceIdType.MESH
LOG2E = math.log2(math.e)


def gelu(v):
    u = v * (math.sqrt(2 / math.pi) + math.sqrt(2 / math.pi) * 0.044715 * (v * v))
    half = 0.5 * v
    return half + half * jnp.tanh(u)


def conv_stack(nat, seg, hbuf, taps_ref, dil_ref, low, high):
    def load(k, _):
        for j in range(8):
            q = k * 8 + j
            for c in range(CT):
                seg[c, q] = nat[c, pl.ds(q, 8, stride=SEG), :]
        return 0

    lax.fori_loop(0, SEG // 8, load, 0)

    def layer(l, _):
        d = dil_ref[l]

        for q in range(0, SEG, 8):
            rows = [seg[c, q : q + 8] for c in range(CT)]
            total = rows[0] * rows[0]
            for c in range(1, CT):
                total = total + rows[c] * rows[c]
            mean = jnp.sum(total, axis=-1, keepdims=True) * (1.0 / C)
            place = (
                lax.broadcasted_iota(jnp.int32, (8, 8, 1), 1) * SEG
                + lax.broadcasted_iota(jnp.int32, (8, 8, 1), 0)
                + q
            )
            scale = jnp.where((place >= low) & (place < high), lax.rsqrt(mean + 1e-06), 0.0)
            for c in range(CT):
                hbuf[c, q + REACH : q + REACH + 8] = rows[c] * scale
        for c in range(CT):
            hbuf[c, 0:REACH] = pltpu.roll(hbuf[c, SEG : SEG + REACH], 1, 1)
            hbuf[c, SEG + REACH : SEG + 2 * REACH] = pltpu.roll(
                hbuf[c, REACH : 2 * REACH], 7, 1
            )
        for c in range(CT):
            cols = slice(c * LANES, (c + 1) * LANES)
            taps = [
                jnp.broadcast_to(taps_ref[l, t : t + 1, cols], (8, LANES))[None]
                for t in range(KSIZE)
            ]

            for q in range(0, SEG, STEP):
                total = taps[0] * hbuf[c, pl.ds(q + REACH - 2 * d, STEP)]
                for t in range(1, KSIZE):
                    total = total + taps[t] * hbuf[c, pl.ds(q + REACH + (t - 2) * d, STEP)]
                seg[c, q : q + STEP] = seg[c, q : q + STEP] + gelu(total)
        return 0

    lax.fori_loop(0, LAYERS, layer, 0)

    def store(k, _):
        for j in range(8):
            q = k * 8 + j
            for c in range(CT):
                nat[c, pl.ds(q, 8, stride=SEG), :] = seg[c, q]
        return 0

    lax.fori_loop(0, SEG // 8, store, 0)


def kernel(
    x_ref, gain_ref, taps_ref, dil_ref, again_ref, wqkv_hbm, wout_hbm, wa_hbm, wb_hbm,
    track_ref, left_ref, rights,
    wqkv, wout, wa, wb, scaled, nat, seg, hbuf, state, halo, near, far, keys, values, q2,
    top, acc, mixed, wsem, send, recv,
):
    block = lax.axis_index("seq")
    core = lax.rem(block, 2)
    sibling = block + 1 - 2 * core
    partner = lax.rem(block + 2, GROUP)
    cross = GROUP - 1 - block

    def remote(src, dst, index, target):
        return pltpu.make_async_remote_copy(
            src_ref=src, dst_ref=dst, send_sem=send.at[index], recv_sem=recv.at[index],
            device_id={"seq": target}, device_id_type=MESH,
        )

    weights = [
        pltpu.make_async_copy(src, dst, wsem.at[i])
        for i, (src, dst) in enumerate(
            ((wqkv_hbm, wqkv), (wout_hbm, wout), (wa_hbm, wa), (wb_hbm, wb))
        )
    ]
    for copy in weights:
        copy.start()
    barrier = pltpu.get_barrier_semaphore()
    for target in (sibling, partner, cross):
        pl.semaphore_signal(barrier, inc=1, device_id={"seq": target}, device_id_type=MESH)

    for t in range(KSIZE):
        product = taps_ref[t] * gain_ref[...]
        for l in range(LAYERS):
            scaled[l, t : t + 1] = product[l : l + 1]
    for c in range(CT):
        nat[c] = x_ref[:, c * LANES : (c + 1) * LANES].astype(F32)
    conv_stack(nat, seg, hbuf, scaled, dil_ref, 0, ROWS)

    def finish(source, target, count):
        rows = [nat[c, source : source + count] for c in range(CT)]
        total = rows[0] * rows[0]
        for c in range(1, CT):
            total = total + rows[c] * rows[c]
        scale = lax.rsqrt(jnp.sum(total, axis=-1, keepdims=True) * (1.0 / C) + 1e-06)
        for c in range(CT):
            cols = slice(c * LANES, (c + 1) * LANES)
            state[c, target : target + count] = rows[c]
            near[0, target : target + count, cols] = (
                rows[c] * scale * again_ref[cols][None]
            ).astype(BF)

    for start in range(EDGE, ROWS - EDGE, 64):
        finish(start, start, 64)
    pl.semaphore_wait(barrier, 3)

    to_left = remote(x_ref.at[pl.ds(0, EDGE)], halo.at[1], 0, lax.rem(block + GROUP - 1, GROUP))
    to_right = remote(
        x_ref.at[pl.ds(ROWS - EDGE, EDGE)], halo.at[0], 1, lax.rem(block + 1, GROUP)
    )
    has_left, has_right = block > 0, block < GROUP - 1

    @pl.when(has_left)
    def _():
        to_left.start()

    @pl.when(has_right)
    def _():
        to_right.start()

    inner = [
        remote(near.at[0, pl.ds(EDGE + i * CHUNK, CHUNK)], far.at[2 * i], 2 + i, partner)
        for i in range(2)
    ]
    inner_near = remote(
        near.at[0, pl.ds(EDGE, 2 * CHUNK)], near.at[1, pl.ds(EDGE, 2 * CHUNK)], 6, sibling
    )
    inner_near.start()
    inner[0].start()

    @pl.when(has_left)
    def _():
        to_right.wait_recv()

    @pl.when(jnp.logical_not(has_left))
    def _():
        halo[0] = jnp.zeros((EDGE, C), BF)

    @pl.when(has_right)
    def _():
        to_left.wait_recv()

    @pl.when(jnp.logical_not(has_right))
    def _():
        halo[1] = jnp.zeros((EDGE, C), BF)

    for c in range(CT):
        cols = slice(c * LANES, (c + 1) * LANES)
        nat[c, 0:EDGE] = halo[0, :, cols].astype(F32)
        nat[c, EDGE : 3 * EDGE] = x_ref[0 : 2 * EDGE, cols].astype(F32)
        nat[c, 3 * EDGE : 5 * EDGE] = x_ref[ROWS - 2 * EDGE :, cols].astype(F32)
        nat[c, 5 * EDGE :] = halo[1, :, cols].astype(F32)
    conv_stack(
        nat, seg, hbuf, scaled, dil_ref,
        jnp.where(has_left, 0, EDGE), jnp.where(has_right, ROWS, ROWS - EDGE),
    )
    finish(EDGE, 0, EDGE)
    finish(ROWS - 2 * EDGE, ROWS - EDGE, EDGE)
    outer = []
    for i, start in enumerate((0, ROWS - EDGE)):
        rows = pl.ds(start, EDGE)
        outer.append(remote(near.at[0, rows], far.at[4, pl.ds(i * EDGE, EDGE)], 4 + i, partner))
        outer.append(remote(near.at[0, rows], near.at[1, rows], 7 + i, sibling))
    outer[1].start()
    outer[3].start()

    weights[0].wait()

    lane = lax.broadcasted_iota(jnp.int32, (1, WIN), 1)

    def project(source, column):
        return jnp.dot(
            source, wqkv[:, column : column + WIN], preferred_element_type=F32
        ).astype(BF)

    def window(p):
        return (p // 2) * (3 * LANES) + (p % 2) * LANES

    for p in range(PAIRS):
        rows = project(near[0], window(p))
        first = (p % 2) * 64
        for i in range(2):
            mine = (lane >= first + 96 * i) & (lane < first + 96 * (i + 1))
            q2[p, i * ROWS : (i + 1) * ROWS] = jnp.where(mine, rows, jnp.zeros_like(rows))

    def spare(p):
        first = (p % 2) * 64
        return (lane < first) | (lane >= first + 192)

    def keys_values(source, place, count):
        for t in range(C // WIN):
            keys[place : place + count, t * WIN : (t + 1) * WIN] = project(source, C + t * WIN)
        for p in range(PAIRS):
            rows = project(source, 2 * C + window(p))
            values[p, place : place + count] = jnp.where(spare(p), jnp.ones_like(rows), rows)

    TILE = 256
    SCALE = LOG2E / math.sqrt(C // HEADS)

    def attend(place, count, fresh):
        for p in range(PAIRS):
            cols = slice(window(p), window(p) + WIN)
            for t in range(2 * ROWS // TILE):
                rows = slice(t * TILE, (t + 1) * TILE)
                scores = lax.dot_general(
                    q2[p, rows], keys[place : place + count, cols],
                    (((1,), (1,)), ((), ())), preferred_element_type=F32,
                )
                pieces = [scores[:, j : j + LANES] for j in range(0, count, LANES)]
                peak = pieces[0]
                for piece in pieces[1:]:
                    peak = jnp.maximum(peak, piece)
                peak = jnp.broadcast_to(jnp.max(peak, axis=-1, keepdims=True), (TILE, LANES))
                if not fresh:
                    old = top[p, rows]
                    peak = jnp.maximum(peak, old)
                top[p, rows] = peak
                probs = jnp.concatenate(
                    [jnp.exp2((piece - peak) * SCALE).astype(BF) for piece in pieces], axis=1
                )
                out = jnp.dot(
                    probs, values[p, place : place + count], preferred_element_type=F32
                )
                if fresh:
                    acc[p, rows] = out
                else:
                    rescale = jnp.exp2((old - peak) * SCALE)
                    for j in range(0, WIN, LANES):
                        acc[p, rows, j : j + LANES] = (
                            acc[p, rows, j : j + LANES] * rescale + out[:, j : j + LANES]
                        )

    inner_near.wait_recv()
    outer[1].wait_recv()
    outer[3].wait_recv()
    keys_values(near[...].reshape(2 * ROWS, C), 0, 2 * ROWS)
    attend(0, 2 * ROWS, True)

    inner[0].wait_send()
    inner[1].start()
    passes = []
    for i in range(3):
        for copy in ([inner[i]] if i < 2 else [outer[0], outer[2]]):
            copy.wait_recv()
        onward = remote(far.at[2 * i], far.at[2 * i + 1], 9 + i, sibling)
        onward.start()
        passes.append(onward)
        if i == 0:
            inner[1].wait_send()
            outer[0].start()
            outer[2].start()
        onward.wait_recv()
        place = 2 * ROWS + 2 * CHUNK * i
        keys_values(far[2 * i : 2 * i + 2].reshape(2 * CHUNK, C), place, 2 * CHUNK)
        attend(place, 2 * CHUNK, False)

    for g in range(2):
        parts = []
        for j in range(2):
            p = 2 * g + j
            both = acc[p] / acc[p, :, 192 * (1 - j) : 192 * (1 - j) + 1]
            first = j * 64
            one = (lane >= first) & (lane < first + 96)
            two = (lane >= first + 96) & (lane < first + 192)
            parts.append(
                jnp.where(one, both[:ROWS], jnp.where(two, both[ROWS:], 0.0))
            )
        base = g * 3 * LANES
        mixed[:, base : base + LANES] = parts[0][:, :LANES].astype(BF)
        mixed[:, base + LANES : base + 2 * LANES] = (
            parts[0][:, LANES:] + parts[1][:, :LANES]
        ).astype(BF)
        mixed[:, base + 2 * LANES : base + 3 * LANES] = parts[1][:, LANES:].astype(BF)

    weights[1].wait()
    squares = jnp.zeros((ROWS // POOL, LANES), F32)
    pools = []
    for t in range(C // WIN):
        product = jnp.dot(
            mixed[...], wout[:, t * WIN : (t + 1) * WIN], preferred_element_type=F32
        )
        for j in range(WIN // LANES):
            c = t * (WIN // LANES) + j
            result = state[c] + product[:, j * LANES : (j + 1) * LANES]
            track_ref[:, c * LANES : (c + 1) * LANES] = result.astype(BF)
            pool = jnp.sum(result.reshape(ROWS // POOL, POOL, LANES), axis=1) * (1.0 / POOL)
            squares = squares + pool * pool
            pools.append(pool)
    scale = lax.rsqrt(jnp.sum(squares, axis=-1, keepdims=True) * (1.0 / C) + 1e-06)
    pooled = jnp.concatenate([pool * scale for pool in pools], axis=1).astype(BF)
    weights[3].wait()
    right = jnp.dot(pooled, wb[...], preferred_element_type=F32).astype(BF)
    rights[pl.ds(block, 1)] = right[None]
    shares = [
        remote(rights.at[block], rights.at[block], 12 + i, target)
        for i, target in enumerate((sibling, partner, cross))
    ]
    for copy in shares[::-1]:
        copy.start()
    weights[2].wait()
    left_ref[...] = jnp.dot(pooled, wa[...], preferred_element_type=F32).astype(BF)
    for copy in shares:
        copy.wait_recv()
    @pl.when(has_left)
    def _():
        to_left.wait_send()

    @pl.when(has_right)
    def _():
        to_right.wait_send()

    for copy in [inner_near] + outer + passes + shares:
        copy.wait_send()


def finale(track_hbm, left_ref, rights_ref, track_out, pair_ref, sem):
    copy = pltpu.make_async_copy(track_hbm, track_out, sem)
    copy.start()
    left = left_ref[...].astype(F32)
    channel = lax.rem(lax.broadcasted_iota(jnp.int32, (PCH, 1, R * PCH), 2), PCH)
    wanted = lax.broadcasted_iota(jnp.int32, (PCH, 1, R * PCH), 0)
    spread = jnp.where(channel == wanted, left[None], 0.0)
    spread = spread.reshape(PCH * (ROWS // POOL), R * PCH).astype(BF)
    every = jnp.concatenate([rights_ref[i].astype(F32) for i in range(GROUP)], axis=0).astype(BF)
    product = lax.dot_general(
        spread, every, (((1,), (1,)), ((), ())), preferred_element_type=F32
    )
    pair_ref[...] = (
        (product * (1.0 / math.sqrt(R))).reshape(PCH, ROWS // POOL, GROUP * ROWS // POOL)
    ).astype(BF)
    copy.wait()


def body(x, conv_gain, conv_kernel, dilation, attn_gain, w_qkv, w_out, w_pair_a, w_pair_b):
    vmem = pl.BlockSpec(memory_space=pltpu.VMEM)
    hbm = pl.BlockSpec(memory_space=pl.ANY)
    track, left, rights = pl.pallas_call(
        kernel,
        out_shape=(
            jax.ShapeDtypeStruct((ROWS, C), BF),
            jax.ShapeDtypeStruct((ROWS // POOL, R * PCH), BF),
            jax.ShapeDtypeStruct((GROUP, ROWS // POOL, R * PCH), BF),
        ),
        in_specs=[vmem, vmem, vmem, pl.BlockSpec(memory_space=pltpu.SMEM), vmem, hbm, hbm, hbm, hbm],
        out_specs=(vmem, vmem, vmem),
        scratch_shapes=[
            pltpu.VMEM(w_qkv.shape, BF),
            pltpu.VMEM(w_out.shape, BF),
            pltpu.VMEM(w_pair_a.shape, BF),
            pltpu.VMEM(w_pair_b.shape, BF),
            pltpu.VMEM((LAYERS, KSIZE, C), F32),
            pltpu.VMEM((CT, ROWS, LANES), F32),
            pltpu.VMEM((CT, SEG, 8, LANES), F32),
            pltpu.VMEM((CT, SEG + 2 * REACH, 8, LANES), F32),
            pltpu.VMEM((CT, ROWS, LANES), F32),
            pltpu.VMEM((2, EDGE, C), BF),
            pltpu.VMEM((2, ROWS, C), BF),
            pltpu.VMEM((6, CHUNK, C), BF),
            pltpu.VMEM((GROUP * ROWS, C), BF),
            pltpu.VMEM((PAIRS, GROUP * ROWS, WIN), BF),
            pltpu.VMEM((PAIRS, 2 * ROWS, WIN), BF),
            pltpu.VMEM((PAIRS, 2 * ROWS, LANES), F32),
            pltpu.VMEM((PAIRS, 2 * ROWS, WIN), F32),
            pltpu.VMEM((ROWS, C), BF),
            pltpu.SemaphoreType.DMA((4,)),
            pltpu.SemaphoreType.DMA((15,)),
            pltpu.SemaphoreType.DMA((15,)),
        ],
        compiler_params=pltpu.CompilerParams(
            collective_id=0, has_side_effects=True, vmem_limit_bytes=60 * 1024 * 1024
        ),
    )(x, conv_gain, conv_kernel.transpose(1, 0, 2), dilation, attn_gain, w_qkv, w_out, w_pair_a, w_pair_b)
    return pl.pallas_call(
        finale,
        out_shape=(
            jax.ShapeDtypeStruct((ROWS, C), BF),
            jax.ShapeDtypeStruct((PCH, ROWS // POOL, GROUP * ROWS // POOL), BF),
        ),
        in_specs=[hbm, vmem, vmem],
        out_specs=(hbm, vmem),
        scratch_shapes=[pltpu.SemaphoreType.DMA],
    )(track, left, rights)


def solution(mesh):
    placed = (P(("batch", "seq"), None), P(), P(), P(), P(), P(), P(), P(), P())
    return jax.shard_map(
        body,
        mesh=mesh,
        in_specs=placed,
        out_specs=(P(("batch", "seq"), None), P("batch", "seq", None)),
        check_vma=False,
    )
```

```python
import math

import jax
import jax.numpy as jnp
from jax import lax
from jax.experimental import pallas as pl
from jax.experimental.pallas import tpu as pltpu
from jax.sharding import PartitionSpec as P

C = 768
HEADS = 8
KSIZE = 5
LAYERS = 4
POOL = 16
PCH = 64
R = 8
ROWS = 384
GROUP = 4
LANES = 128
CT = C // LANES
REACH = 16
EDGE = LAYERS * REACH
SEG = ROWS // 8
STEP = 8
CHUNK = 128
PAIRS = HEADS // 2
WIN = 256
BF = jnp.bfloat16
F32 = jnp.float32
MESH = pl.DeviceIdType.MESH
LOG2E = math.log2(math.e)


def gelu(v):
    u = v * (math.sqrt(2 / math.pi) + math.sqrt(2 / math.pi) * 0.044715 * (v * v))
    half = 0.5 * v
    return half + half * jnp.tanh(u)


def conv_stack(nat, seg, hbuf, taps_ref, dil_ref, low, high):
    def load(k, _):
        for j in range(8):
            q = k * 8 + j
            for c in range(CT):
                seg[c, q] = nat[c, pl.ds(q, 8, stride=SEG), :]
        return 0

    lax.fori_loop(0, SEG // 8, load, 0)

    def layer(l, _):
        d = dil_ref[l]

        for q in range(0, SEG, 8):
            rows = [seg[c, q : q + 8] for c in range(CT)]
            total = rows[0] * rows[0]
            for c in range(1, CT):
                total = total + rows[c] * rows[c]
            mean = jnp.sum(total, axis=-1, keepdims=True) * (1.0 / C)
            place = (
                lax.broadcasted_iota(jnp.int32, (8, 8, 1), 1) * SEG
                + lax.broadcasted_iota(jnp.int32, (8, 8, 1), 0)
                + q
            )
            scale = jnp.where((place >= low) & (place < high), lax.rsqrt(mean + 1e-06), 0.0)
            for c in range(CT):
                hbuf[c, q + REACH : q + REACH + 8] = rows[c] * scale
        for c in range(CT):
            hbuf[c, 0:REACH] = pltpu.roll(hbuf[c, SEG : SEG + REACH], 1, 1)
            hbuf[c, SEG + REACH : SEG + 2 * REACH] = pltpu.roll(
                hbuf[c, REACH : 2 * REACH], 7, 1
            )
        for c in range(CT):
            cols = slice(c * LANES, (c + 1) * LANES)
            taps = [
                jnp.broadcast_to(taps_ref[l, t : t + 1, cols], (8, LANES))[None]
                for t in range(KSIZE)
            ]

            for q in range(0, SEG, STEP):
                total = taps[0] * hbuf[c, pl.ds(q + REACH - 2 * d, STEP)]
                for t in range(1, KSIZE):
                    total = total + taps[t] * hbuf[c, pl.ds(q + REACH + (t - 2) * d, STEP)]
                seg[c, q : q + STEP] = seg[c, q : q + STEP] + gelu(total)
        return 0

    lax.fori_loop(0, LAYERS, layer, 0)

    def store(k, _):
        for j in range(8):
            q = k * 8 + j
            for c in range(CT):
                nat[c, pl.ds(q, 8, stride=SEG), :] = seg[c, q]
        return 0

    lax.fori_loop(0, SEG // 8, store, 0)


def kernel(
    x_ref, gain_ref, taps_ref, dil_ref, again_ref, wqkv_hbm, wout_hbm, wa_hbm, wb_hbm,
    track_ref, left_ref, rights,
    wqkv, wout, wa, wb, scaled, nat, seg, hbuf, state, halo, near, far, keys, values, q2,
    top, acc, mixed, wsem, send, recv,
):
    block = lax.axis_index("seq")
    core = lax.rem(block, 2)
    sibling = block + 1 - 2 * core
    partner = lax.rem(block + 2, GROUP)
    cross = GROUP - 1 - block

    def remote(src, dst, index, target):
        return pltpu.make_async_remote_copy(
            src_ref=src, dst_ref=dst, send_sem=send.at[index], recv_sem=recv.at[index],
            device_id={"seq": target}, device_id_type=MESH,
        )

    weights = [
        pltpu.make_async_copy(src, dst, wsem.at[i])
        for i, (src, dst) in enumerate(
            ((wqkv_hbm, wqkv), (wout_hbm, wout), (wa_hbm, wa), (wb_hbm, wb))
        )
    ]
    for copy in weights:
        copy.start()
    barrier = pltpu.get_barrier_semaphore()
    for target in (sibling, partner, cross):
        pl.semaphore_signal(barrier, inc=1, device_id={"seq": target}, device_id_type=MESH)

    for t in range(KSIZE):
        product = taps_ref[t] * gain_ref[...]
        for l in range(LAYERS):
            scaled[l, t : t + 1] = product[l : l + 1]
    for c in range(CT):
        nat[c] = x_ref[:, c * LANES : (c + 1) * LANES].astype(F32)
    conv_stack(nat, seg, hbuf, scaled, dil_ref, 0, ROWS)

    def finish(source, target, count):
        rows = [nat[c, source : source + count] for c in range(CT)]
        total = rows[0] * rows[0]
        for c in range(1, CT):
            total = total + rows[c] * rows[c]
        scale = lax.rsqrt(jnp.sum(total, axis=-1, keepdims=True) * (1.0 / C) + 1e-06)
        for c in range(CT):
            cols = slice(c * LANES, (c + 1) * LANES)
            state[c, target : target + count] = rows[c]
            near[0, target : target + count, cols] = (
                rows[c] * scale * again_ref[cols][None]
            ).astype(BF)

    for start in range(EDGE, ROWS - EDGE, 64):
        finish(start, start, 64)
    pl.semaphore_wait(barrier, 3)

    to_left = remote(x_ref.at[pl.ds(0, EDGE)], halo.at[1], 0, lax.rem(block + GROUP - 1, GROUP))
    to_right = remote(
        x_ref.at[pl.ds(ROWS - EDGE, EDGE)], halo.at[0], 1, lax.rem(block + 1, GROUP)
    )
    has_left, has_right = block > 0, block < GROUP - 1

    @pl.when(has_left)
    def _():
        to_left.start()

    @pl.when(has_right)
    def _():
        to_right.start()

    inner = [
        remote(near.at[0, pl.ds(EDGE + i * CHUNK, CHUNK)], far.at[2 * i], 2 + i, partner)
        for i in range(2)
    ]
    inner_near = remote(
        near.at[0, pl.ds(EDGE, 2 * CHUNK)], near.at[1, pl.ds(EDGE, 2 * CHUNK)], 6, sibling
    )
    inner_near.start()
    inner[0].start()
    inner[1].start()

    @pl.when(has_left)
    def _():
        to_right.wait_recv()

    @pl.when(jnp.logical_not(has_left))
    def _():
        halo[0] = jnp.zeros((EDGE, C), BF)

    @pl.when(has_right)
    def _():
        to_left.wait_recv()

    @pl.when(jnp.logical_not(has_right))
    def _():
        halo[1] = jnp.zeros((EDGE, C), BF)

    for c in range(CT):
        cols = slice(c * LANES, (c + 1) * LANES)
        nat[c, 0:EDGE] = halo[0, :, cols].astype(F32)
        nat[c, EDGE : 3 * EDGE] = x_ref[0 : 2 * EDGE, cols].astype(F32)
        nat[c, 3 * EDGE : 5 * EDGE] = x_ref[ROWS - 2 * EDGE :, cols].astype(F32)
        nat[c, 5 * EDGE :] = halo[1, :, cols].astype(F32)
    conv_stack(
        nat, seg, hbuf, scaled, dil_ref,
        jnp.where(has_left, 0, EDGE), jnp.where(has_right, ROWS, ROWS - EDGE),
    )
    finish(EDGE, 0, EDGE)
    finish(ROWS - 2 * EDGE, ROWS - EDGE, EDGE)
    outer = []
    for i, start in enumerate((0, ROWS - EDGE)):
        rows = pl.ds(start, EDGE)
        outer.append(remote(near.at[0, rows], far.at[4, pl.ds(i * EDGE, EDGE)], 4 + i, partner))
        outer.append(remote(near.at[0, rows], near.at[1, rows], 7 + i, sibling))
    outer[1].start()
    outer[3].start()

    weights[0].wait()

    lane = lax.broadcasted_iota(jnp.int32, (1, WIN), 1)

    def project(source, column):
        return jnp.dot(
            source, wqkv[:, column : column + WIN], preferred_element_type=F32
        ).astype(BF)

    def window(p):
        return (p // 2) * (3 * LANES) + (p % 2) * LANES

    for p in range(PAIRS):
        rows = project(near[0], window(p))
        first = (p % 2) * 64
        for i in range(2):
            mine = (lane >= first + 96 * i) & (lane < first + 96 * (i + 1))
            q2[p, i * ROWS : (i + 1) * ROWS] = jnp.where(mine, rows, jnp.zeros_like(rows))

    def spare(p):
        first = (p % 2) * 64
        return (lane < first) | (lane >= first + 192)

    def keys_values(source, place, count):
        for t in range(C // WIN):
            keys[place : place + count, t * WIN : (t + 1) * WIN] = project(source, C + t * WIN)
        for p in range(PAIRS):
            rows = project(source, 2 * C + window(p))
            values[p, place : place + count] = jnp.where(spare(p), jnp.ones_like(rows), rows)

    TILE = 256
    SCALE = LOG2E / math.sqrt(C // HEADS)

    def attend(place, count, fresh):
        for p in range(PAIRS):
            cols = slice(window(p), window(p) + WIN)
            for t in range(2 * ROWS // TILE):
                rows = slice(t * TILE, (t + 1) * TILE)
                scores = lax.dot_general(
                    q2[p, rows], keys[place : place + count, cols],
                    (((1,), (1,)), ((), ())), preferred_element_type=F32,
                )
                pieces = [scores[:, j : j + LANES] for j in range(0, count, LANES)]
                peak = pieces[0]
                for piece in pieces[1:]:
                    peak = jnp.maximum(peak, piece)
                peak = jnp.broadcast_to(jnp.max(peak, axis=-1, keepdims=True), (TILE, LANES))
                if not fresh:
                    old = top[p, rows]
                    peak = jnp.maximum(peak, old)
                top[p, rows] = peak
                probs = jnp.concatenate(
                    [jnp.exp2((piece - peak) * SCALE).astype(BF) for piece in pieces], axis=1
                )
                out = jnp.dot(
                    probs, values[p, place : place + count], preferred_element_type=F32
                )
                if fresh:
                    acc[p, rows] = out
                else:
                    rescale = jnp.exp2((old - peak) * SCALE)
                    for j in range(0, WIN, LANES):
                        acc[p, rows, j : j + LANES] = (
                            acc[p, rows, j : j + LANES] * rescale + out[:, j : j + LANES]
                        )

    inner_near.wait_recv()
    outer[1].wait_recv()
    outer[3].wait_recv()
    keys_values(near[...].reshape(2 * ROWS, C), 0, 2 * ROWS)
    attend(0, 2 * ROWS, True)

    inner[0].wait_send()
    outer[0].start()
    outer[2].start()
    passes = []
    for i in range(3):
        for copy in ([inner[i]] if i < 2 else [outer[0], outer[2]]):
            copy.wait_recv()
        onward = remote(far.at[2 * i], far.at[2 * i + 1], 9 + i, sibling)
        onward.start()
        passes.append(onward)
        onward.wait_recv()
        place = 2 * ROWS + 2 * CHUNK * i
        keys_values(far[2 * i : 2 * i + 2].reshape(2 * CHUNK, C), place, 2 * CHUNK)
        attend(place, 2 * CHUNK, False)

    for g in range(2):
        parts = []
        for j in range(2):
            p = 2 * g + j
            both = acc[p] * (1.0 / acc[p, :, 192 * (1 - j) : 192 * (1 - j) + 1])
            first = j * 64
            one = (lane >= first) & (lane < first + 96)
            two = (lane >= first + 96) & (lane < first + 192)
            parts.append(
                jnp.where(one, both[:ROWS], jnp.where(two, both[ROWS:], 0.0))
            )
        base = g * 3 * LANES
        mixed[:, base : base + LANES] = parts[0][:, :LANES].astype(BF)
        mixed[:, base + LANES : base + 2 * LANES] = (
            parts[0][:, LANES:] + parts[1][:, :LANES]
        ).astype(BF)
        mixed[:, base + 2 * LANES : base + 3 * LANES] = parts[1][:, LANES:].astype(BF)

    weights[1].wait()
    squares = jnp.zeros((ROWS // POOL, LANES), F32)
    pools = []
    for t in range(C // WIN):
        product = jnp.dot(
            mixed[...], wout[:, t * WIN : (t + 1) * WIN], preferred_element_type=F32
        )
        for j in range(WIN // LANES):
            c = t * (WIN // LANES) + j
            result = state[c] + product[:, j * LANES : (j + 1) * LANES]
            track_ref[:, c * LANES : (c + 1) * LANES] = result.astype(BF)
            pool = jnp.sum(result.reshape(ROWS // POOL, POOL, LANES), axis=1) * (1.0 / POOL)
            squares = squares + pool * pool
            pools.append(pool)
    scale = lax.rsqrt(jnp.sum(squares, axis=-1, keepdims=True) * (1.0 / C) + 1e-06)
    pooled = jnp.concatenate([pool * scale for pool in pools], axis=1).astype(BF)
    weights[3].wait()
    right = jnp.dot(pooled, wb[...], preferred_element_type=F32).astype(BF)
    rights[pl.ds(block, 1)] = right[None]
    shares = [
        remote(rights.at[block], rights.at[block], 12 + i, target)
        for i, target in enumerate((sibling, partner, cross))
    ]
    for copy in shares[::-1]:
        copy.start()
    weights[2].wait()
    left_ref[...] = jnp.dot(pooled, wa[...], preferred_element_type=F32).astype(BF)
    for copy in shares:
        copy.wait_recv()
    @pl.when(has_left)
    def _():
        to_left.wait_send()

    @pl.when(has_right)
    def _():
        to_right.wait_send()

    for copy in [inner[1], inner_near] + outer + passes + shares:
        copy.wait_send()


def finale(track_ref, left_ref, rights_ref, track_out, pair_ref, sem):
    copy = pltpu.make_async_copy(track_ref, track_out, sem)
    copy.start()
    left = left_ref[...].astype(F32)
    channel = lax.rem(lax.broadcasted_iota(jnp.int32, (PCH, 1, R * PCH), 2), PCH)
    wanted = lax.broadcasted_iota(jnp.int32, (PCH, 1, R * PCH), 0)
    spread = jnp.where(channel == wanted, left[None], 0.0)
    spread = spread.reshape(PCH * (ROWS // POOL), R * PCH).astype(BF)
    every = jnp.concatenate([rights_ref[i].astype(F32) for i in range(GROUP)], axis=0).astype(BF)
    product = lax.dot_general(
        spread, every, (((1,), (1,)), ((), ())), preferred_element_type=F32
    )
    pair_ref[...] = (
        (product * (1.0 / math.sqrt(R))).reshape(PCH, ROWS // POOL, GROUP * ROWS // POOL)
    ).astype(BF)
    copy.wait()


def body(x, conv_gain, conv_kernel, dilation, attn_gain, w_qkv, w_out, w_pair_a, w_pair_b):
    vmem = pl.BlockSpec(memory_space=pltpu.VMEM)
    hbm = pl.BlockSpec(memory_space=pl.ANY)
    track, left, rights = pl.pallas_call(
        kernel,
        out_shape=(
            jax.ShapeDtypeStruct((ROWS, C), BF),
            jax.ShapeDtypeStruct((ROWS // POOL, R * PCH), BF),
            jax.ShapeDtypeStruct((GROUP, ROWS // POOL, R * PCH), BF),
        ),
        in_specs=[vmem, vmem, vmem, pl.BlockSpec(memory_space=pltpu.SMEM), vmem, hbm, hbm, hbm, hbm],
        out_specs=(vmem, vmem, vmem),
        scratch_shapes=[
            pltpu.VMEM(w_qkv.shape, BF),
            pltpu.VMEM(w_out.shape, BF),
            pltpu.VMEM(w_pair_a.shape, BF),
            pltpu.VMEM(w_pair_b.shape, BF),
            pltpu.VMEM((LAYERS, KSIZE, C), F32),
            pltpu.VMEM((CT, ROWS, LANES), F32),
            pltpu.VMEM((CT, SEG, 8, LANES), F32),
            pltpu.VMEM((CT, SEG + 2 * REACH, 8, LANES), F32),
            pltpu.VMEM((CT, ROWS, LANES), F32),
            pltpu.VMEM((2, EDGE, C), BF),
            pltpu.VMEM((2, ROWS, C), BF),
            pltpu.VMEM((6, CHUNK, C), BF),
            pltpu.VMEM((GROUP * ROWS, C), BF),
            pltpu.VMEM((PAIRS, GROUP * ROWS, WIN), BF),
            pltpu.VMEM((PAIRS, 2 * ROWS, WIN), BF),
            pltpu.VMEM((PAIRS, 2 * ROWS, LANES), F32),
            pltpu.VMEM((PAIRS, 2 * ROWS, WIN), F32),
            pltpu.VMEM((ROWS, C), BF),
            pltpu.SemaphoreType.DMA((4,)),
            pltpu.SemaphoreType.DMA((15,)),
            pltpu.SemaphoreType.DMA((15,)),
        ],
        compiler_params=pltpu.CompilerParams(
            collective_id=0, has_side_effects=True, vmem_limit_bytes=60 * 1024 * 1024
        ),
    )(x, conv_gain, conv_kernel.transpose(1, 0, 2), dilation, attn_gain, w_qkv, w_out, w_pair_a, w_pair_b)
    return pl.pallas_call(
        finale,
        out_shape=(
            jax.ShapeDtypeStruct((ROWS, C), BF),
            jax.ShapeDtypeStruct((PCH, ROWS // POOL, GROUP * ROWS // POOL), BF),
        ),
        in_specs=[vmem, vmem, vmem],
        out_specs=(hbm, vmem),
        scratch_shapes=[pltpu.SemaphoreType.DMA],
    )(track, left, rights)


def solution(mesh):
    placed = (P(("batch", "seq"), None), P(), P(), P(), P(), P(), P(), P(), P())
    return jax.shard_map(
        body,
        mesh=mesh,
        in_specs=placed,
        out_specs=(P(("batch", "seq"), None), P("batch", "seq", None)),
        check_vma=False,
    )
```

```python
import math

import jax
import jax.numpy as jnp
from jax import lax
from jax.experimental import pallas as pl
from jax.experimental.pallas import tpu as pltpu
from jax.sharding import PartitionSpec as P

C = 768
HEADS = 8
KSIZE = 5
LAYERS = 4
POOL = 16
PCH = 64
R = 8
ROWS = 384
GROUP = 4
LANES = 128
CT = C // LANES
REACH = 16
EDGE = LAYERS * REACH
SEG = ROWS // 8
STEP = 8
CHUNK = 128
PAIRS = HEADS // 2
WIN = 256
BF = jnp.bfloat16
F32 = jnp.float32
MESH = pl.DeviceIdType.MESH
ROOT = math.sqrt(2 / math.pi)
LOG2E = math.log2(math.e)


def gelu_of_double(half):
    u = half * (2 * ROOT + 8 * 0.044715 * ROOT * (half * half))
    return half + half * jnp.tanh(u)


def conv_stack(nat, seg, hbuf, taps_ref, dil_ref, low, high):
    def load(k, _):
        for j in range(8):
            q = k * 8 + j
            for c in range(CT):
                seg[c, q] = nat[c, pl.ds(q, 8, stride=SEG), :]
        return 0

    lax.fori_loop(0, SEG // 8, load, 0)

    def layer(l, _):
        d = dil_ref[l]

        for q in range(0, SEG, 8):
            rows = [seg[c, q : q + 8] for c in range(CT)]
            total = rows[0] * rows[0]
            for c in range(1, CT):
                total = total + rows[c] * rows[c]
            mean = jnp.sum(total, axis=-1, keepdims=True) * (1.0 / C)
            place = (
                lax.broadcasted_iota(jnp.int32, (8, 8, 1), 1) * SEG
                + lax.broadcasted_iota(jnp.int32, (8, 8, 1), 0)
                + q
            )
            scale = jnp.where((place >= low) & (place < high), lax.rsqrt(mean + 1e-06), 0.0)
            for c in range(CT):
                hbuf[c, q + REACH : q + REACH + 8] = rows[c] * scale
        for c in range(CT):
            hbuf[c, 0:REACH] = pltpu.roll(hbuf[c, SEG : SEG + REACH], 1, 1)
            hbuf[c, SEG + REACH : SEG + 2 * REACH] = pltpu.roll(
                hbuf[c, REACH : 2 * REACH], 7, 1
            )
        for c in range(CT):
            cols = slice(c * LANES, (c + 1) * LANES)
            taps = [
                jnp.broadcast_to(taps_ref[l, t : t + 1, cols], (8, LANES))[None]
                for t in range(KSIZE)
            ]

            for q in range(0, SEG, STEP):
                total = taps[0] * hbuf[c, pl.ds(q + REACH - 2 * d, STEP)]
                for t in range(1, KSIZE):
                    total = total + taps[t] * hbuf[c, pl.ds(q + REACH + (t - 2) * d, STEP)]
                seg[c, q : q + STEP] = seg[c, q : q + STEP] + gelu_of_double(total)
        return 0

    lax.fori_loop(0, LAYERS, layer, 0)

    def store(k, _):
        for j in range(8):
            q = k * 8 + j
            for c in range(CT):
                nat[c, pl.ds(q, 8, stride=SEG), :] = seg[c, q]
        return 0

    lax.fori_loop(0, SEG // 8, store, 0)


def kernel(
    x_ref, gain_ref, taps_ref, dil_ref, again_ref, wqkv_hbm, wout_hbm, wa_hbm, wb_hbm,
    track_ref, left_ref, rights,
    wqkv, wout, wa, wb, scaled, nat, seg, hbuf, state, halo, near, far, keys, values, q2,
    top, acc, mixed, wsem, send, recv,
):
    block = lax.axis_index("seq")
    core = lax.rem(block, 2)
    sibling = block + 1 - 2 * core
    partner = lax.rem(block + 2, GROUP)
    cross = GROUP - 1 - block

    def remote(src, dst, index, target):
        return pltpu.make_async_remote_copy(
            src_ref=src, dst_ref=dst, send_sem=send.at[index], recv_sem=recv.at[index],
            device_id={"seq": target}, device_id_type=MESH,
        )

    weights = [
        pltpu.make_async_copy(src, dst, wsem.at[i])
        for i, (src, dst) in enumerate(
            ((wqkv_hbm, wqkv), (wout_hbm, wout), (wa_hbm, wa), (wb_hbm, wb))
        )
    ]
    for copy in weights:
        copy.start()
    barrier = pltpu.get_barrier_semaphore()
    for target in (sibling, partner, cross):
        pl.semaphore_signal(barrier, inc=1, device_id={"seq": target}, device_id_type=MESH)

    to_left = remote(x_ref.at[pl.ds(0, EDGE)], halo.at[1], 0, lax.rem(block + GROUP - 1, GROUP))
    to_right = remote(
        x_ref.at[pl.ds(ROWS - EDGE, EDGE)], halo.at[0], 1, lax.rem(block + 1, GROUP)
    )
    has_left, has_right = block > 0, block < GROUP - 1

    upper = block >= GROUP // 2

    def meet():
        pl.semaphore_wait(barrier, 3)

        @pl.when(has_left)
        def _():
            to_left.start()

        @pl.when(has_right)
        def _():
            to_right.start()

    @pl.when(upper)
    def _():
        meet()

    for t in range(KSIZE):
        product = (taps_ref[t] * gain_ref[...]) * 0.5
        for l in range(LAYERS):
            scaled[l, t : t + 1] = product[l : l + 1]
    for c in range(CT):
        nat[c] = x_ref[:, c * LANES : (c + 1) * LANES].astype(F32)
    conv_stack(nat, seg, hbuf, scaled, dil_ref, 0, ROWS)

    def finish(source, target, count):
        rows = [nat[c, source : source + count] for c in range(CT)]
        total = rows[0] * rows[0]
        for c in range(1, CT):
            total = total + rows[c] * rows[c]
        scale = lax.rsqrt(jnp.sum(total, axis=-1, keepdims=True) * (1.0 / C) + 1e-06)
        for c in range(CT):
            cols = slice(c * LANES, (c + 1) * LANES)
            state[c, target : target + count] = rows[c]
            near[0, target : target + count, cols] = (
                rows[c] * scale * again_ref[cols][None]
            ).astype(BF)

    for start in range(EDGE, ROWS - EDGE, 64):
        finish(start, start, 64)
    @pl.when(jnp.logical_not(upper))
    def _():
        meet()

    inner = [
        remote(near.at[0, pl.ds(EDGE + i * CHUNK, CHUNK)], far.at[2 * i], 2 + i, partner)
        for i in range(2)
    ]
    inner_near = remote(
        near.at[0, pl.ds(EDGE, 2 * CHUNK)], near.at[1, pl.ds(EDGE, 2 * CHUNK)], 6, sibling
    )
    inner_near.start()
    inner[0].start()
    inner[1].start()

    @pl.when(has_left)
    def _():
        to_right.wait_recv()

    @pl.when(jnp.logical_not(has_left))
    def _():
        halo[0] = jnp.zeros((EDGE, C), BF)

    @pl.when(has_right)
    def _():
        to_left.wait_recv()

    @pl.when(jnp.logical_not(has_right))
    def _():
        halo[1] = jnp.zeros((EDGE, C), BF)

    for c in range(CT):
        cols = slice(c * LANES, (c + 1) * LANES)
        nat[c, 0:EDGE] = halo[0, :, cols].astype(F32)
        nat[c, EDGE : 3 * EDGE] = x_ref[0 : 2 * EDGE, cols].astype(F32)
        nat[c, 3 * EDGE : 5 * EDGE] = x_ref[ROWS - 2 * EDGE :, cols].astype(F32)
        nat[c, 5 * EDGE :] = halo[1, :, cols].astype(F32)
    conv_stack(
        nat, seg, hbuf, scaled, dil_ref,
        jnp.where(has_left, 0, EDGE), jnp.where(has_right, ROWS, ROWS - EDGE),
    )
    finish(EDGE, 0, EDGE)
    finish(ROWS - 2 * EDGE, ROWS - EDGE, EDGE)
    outer = []
    for i, start in enumerate((0, ROWS - EDGE)):
        rows = pl.ds(start, EDGE)
        outer.append(remote(near.at[0, rows], far.at[4, pl.ds(i * EDGE, EDGE)], 4 + i, partner))
        outer.append(remote(near.at[0, rows], near.at[1, rows], 7 + i, sibling))
    for copy in outer:
        copy.start()

    weights[0].wait()

    lane = lax.broadcasted_iota(jnp.int32, (1, WIN), 1)

    def project(source, column):
        return jnp.dot(
            source, wqkv[:, column : column + WIN], preferred_element_type=F32
        ).astype(BF)

    def window(p):
        return (p // 2) * (3 * LANES) + (p % 2) * LANES

    for p in range(PAIRS):
        rows = project(near[0], window(p))
        first = (p % 2) * 64
        for i in range(2):
            mine = (lane >= first + 96 * i) & (lane < first + 96 * (i + 1))
            q2[p, i * ROWS : (i + 1) * ROWS] = jnp.where(mine, rows, jnp.zeros_like(rows))

    def spare(p):
        first = (p % 2) * 64
        return (lane < first) | (lane >= first + 192)

    def keys_values(source, place, count):
        for t in range(C // WIN):
            keys[place : place + count, t * WIN : (t + 1) * WIN] = project(source, C + t * WIN)
        for p in range(PAIRS):
            rows = project(source, 2 * C + window(p))
            values[p, place : place + count] = jnp.where(spare(p), jnp.ones_like(rows), rows)

    TILE = 256
    SCALE = LOG2E / math.sqrt(C // HEADS)

    def attend(place, count, fresh):
        for p in range(PAIRS):
            cols = slice(window(p), window(p) + WIN)
            for t in range(2 * ROWS // TILE):
                rows = slice(t * TILE, (t + 1) * TILE)
                scores = lax.dot_general(
                    q2[p, rows], keys[place : place + count, cols],
                    (((1,), (1,)), ((), ())), preferred_element_type=F32,
                )
                pieces = [scores[:, j : j + LANES] for j in range(0, count, LANES)]
                peak = pieces[0]
                for piece in pieces[1:]:
                    peak = jnp.maximum(peak, piece)
                peak = jnp.broadcast_to(jnp.max(peak, axis=-1, keepdims=True), (TILE, LANES))
                if not fresh:
                    old = top[p, rows]
                    peak = jnp.maximum(peak, old)
                top[p, rows] = peak
                probs = jnp.concatenate(
                    [jnp.exp2((piece - peak) * SCALE).astype(BF) for piece in pieces], axis=1
                )
                out = jnp.dot(
                    probs, values[p, place : place + count], preferred_element_type=F32
                )
                if fresh:
                    acc[p, rows] = out
                else:
                    rescale = jnp.exp2((old - peak) * SCALE)
                    for j in range(0, WIN, LANES):
                        acc[p, rows, j : j + LANES] = (
                            acc[p, rows, j : j + LANES] * rescale + out[:, j : j + LANES]
                        )

    inner_near.wait_recv()
    outer[1].wait_recv()
    outer[3].wait_recv()
    keys_values(near[...].reshape(2 * ROWS, C), 0, 2 * ROWS)
    attend(0, 2 * ROWS, True)

    passes = []
    for i in range(3):
        place = 2 * ROWS + 2 * CHUNK * i
        onward = remote(far.at[2 * i], far.at[2 * i + 1], 9 + i, sibling)
        for copy in ([inner[i]] if i < 2 else [outer[0], outer[2]]):
            copy.wait_recv()
        onward.start()
        passes.append(onward)
        if i < 2:
            onward.wait_recv()
            keys_values(far[2 * i : 2 * i + 2].reshape(2 * CHUNK, C), place, 2 * CHUNK)
        else:
            keys_values(far[2 * i], place, CHUNK)
            onward.wait_recv()
            keys_values(far[2 * i + 1], place + CHUNK, CHUNK)
        attend(place, 2 * CHUNK, False)

    for g in range(2):
        parts = []
        for j in range(2):
            p = 2 * g + j
            both = acc[p] * (1.0 / acc[p, :, 192 * (1 - j) : 192 * (1 - j) + 1])
            first = j * 64
            one = (lane >= first) & (lane < first + 96)
            two = (lane >= first + 96) & (lane < first + 192)
            parts.append(
                jnp.where(one, both[:ROWS], jnp.where(two, both[ROWS:], 0.0))
            )
        base = g * 3 * LANES
        mixed[:, base : base + LANES] = parts[0][:, :LANES].astype(BF)
        mixed[:, base + LANES : base + 2 * LANES] = (
            parts[0][:, LANES:] + parts[1][:, :LANES]
        ).astype(BF)
        mixed[:, base + 2 * LANES : base + 3 * LANES] = parts[1][:, LANES:].astype(BF)

    weights[1].wait()
    squares = jnp.zeros((ROWS // POOL, LANES), F32)
    pools = []
    for t in range(C // WIN):
        product = jnp.dot(
            mixed[...], wout[:, t * WIN : (t + 1) * WIN], preferred_element_type=F32
        )
        for j in range(WIN // LANES):
            c = t * (WIN // LANES) + j
            result = state[c] + product[:, j * LANES : (j + 1) * LANES]
            track_ref[:, c * LANES : (c + 1) * LANES] = result.astype(BF)
            pool = jnp.sum(result.reshape(ROWS // POOL, POOL, LANES), axis=1) * (1.0 / POOL)
            squares = squares + pool * pool
            pools.append(pool)
    scale = lax.rsqrt(jnp.sum(squares, axis=-1, keepdims=True) * (1.0 / C) + 1e-06)
    pooled = jnp.concatenate([pool * scale for pool in pools], axis=1).astype(BF)
    weights[3].wait()
    right = jnp.dot(pooled, wb[...], preferred_element_type=F32).astype(BF)
    rights[pl.ds(block, 1)] = right[None]
    shares = [
        remote(rights.at[block], rights.at[block], 12 + i, target)
        for i, target in enumerate((sibling, partner, cross))
    ]
    for copy in shares[::-1]:
        copy.start()
    weights[2].wait()
    left_ref[...] = jnp.dot(pooled, wa[...], preferred_element_type=F32).astype(BF)
    for copy in shares:
        copy.wait_recv()
    @pl.when(has_left)
    def _():
        to_left.wait_send()

    @pl.when(has_right)
    def _():
        to_right.wait_send()

    for copy in inner + [inner_near] + outer + passes + shares:
        copy.wait_send()


def finale(track_ref, left_ref, rights_ref, track_out, pair_ref, sem):
    copy = pltpu.make_async_copy(track_ref, track_out, sem)
    copy.start()
    left = left_ref[...].astype(F32)
    channel = lax.rem(lax.broadcasted_iota(jnp.int32, (PCH, 1, R * PCH), 2), PCH)
    wanted = lax.broadcasted_iota(jnp.int32, (PCH, 1, R * PCH), 0)
    spread = jnp.where(channel == wanted, left[None], 0.0)
    spread = spread.reshape(PCH * (ROWS // POOL), R * PCH).astype(BF)
    every = jnp.concatenate([rights_ref[i].astype(F32) for i in range(GROUP)], axis=0).astype(BF)
    product = lax.dot_general(
        spread, every, (((1,), (1,)), ((), ())), preferred_element_type=F32
    )
    pair_ref[...] = (
        (product * (1.0 / math.sqrt(R))).reshape(PCH, ROWS // POOL, GROUP * ROWS // POOL)
    ).astype(BF)
    copy.wait()


def body(x, conv_gain, conv_kernel, dilation, attn_gain, w_qkv, w_out, w_pair_a, w_pair_b):
    vmem = pl.BlockSpec(memory_space=pltpu.VMEM)
    hbm = pl.BlockSpec(memory_space=pl.ANY)
    track, left, rights = pl.pallas_call(
        kernel,
        out_shape=(
            jax.ShapeDtypeStruct((ROWS, C), BF),
            jax.ShapeDtypeStruct((ROWS // POOL, R * PCH), BF),
            jax.ShapeDtypeStruct((GROUP, ROWS // POOL, R * PCH), BF),
        ),
        in_specs=[vmem, vmem, vmem, pl.BlockSpec(memory_space=pltpu.SMEM), vmem, hbm, hbm, hbm, hbm],
        out_specs=(vmem, vmem, vmem),
        scratch_shapes=[
            pltpu.VMEM(w_qkv.shape, BF),
            pltpu.VMEM(w_out.shape, BF),
            pltpu.VMEM(w_pair_a.shape, BF),
            pltpu.VMEM(w_pair_b.shape, BF),
            pltpu.VMEM((LAYERS, KSIZE, C), F32),
            pltpu.VMEM((CT, ROWS, LANES), F32),
            pltpu.VMEM((CT, SEG, 8, LANES), F32),
            pltpu.VMEM((CT, SEG + 2 * REACH, 8, LANES), F32),
            pltpu.VMEM((CT, ROWS, LANES), F32),
            pltpu.VMEM((2, EDGE, C), BF),
            pltpu.VMEM((2, ROWS, C), BF),
            pltpu.VMEM((6, CHUNK, C), BF),
            pltpu.VMEM((GROUP * ROWS, C), BF),
            pltpu.VMEM((PAIRS, GROUP * ROWS, WIN), BF),
            pltpu.VMEM((PAIRS, 2 * ROWS, WIN), BF),
            pltpu.VMEM((PAIRS, 2 * ROWS, LANES), F32),
            pltpu.VMEM((PAIRS, 2 * ROWS, WIN), F32),
            pltpu.VMEM((ROWS, C), BF),
            pltpu.SemaphoreType.DMA((4,)),
            pltpu.SemaphoreType.DMA((15,)),
            pltpu.SemaphoreType.DMA((15,)),
        ],
        compiler_params=pltpu.CompilerParams(
            collective_id=0, has_side_effects=True, vmem_limit_bytes=60 * 1024 * 1024
        ),
    )(x, conv_gain, conv_kernel.transpose(1, 0, 2), dilation, attn_gain, w_qkv, w_out, w_pair_a, w_pair_b)
    return pl.pallas_call(
        finale,
        out_shape=(
            jax.ShapeDtypeStruct((ROWS, C), BF),
            jax.ShapeDtypeStruct((PCH, ROWS // POOL, GROUP * ROWS // POOL), BF),
        ),
        in_specs=[vmem, vmem, vmem],
        out_specs=(hbm, vmem),
        scratch_shapes=[pltpu.SemaphoreType.DMA],
    )(track, left, rights)


def solution(mesh):
    placed = (P(("batch", "seq"), None), P(), P(), P(), P(), P(), P(), P(), P())
    return jax.shard_map(
        body,
        mesh=mesh,
        in_specs=placed,
        out_specs=(P(("batch", "seq"), None), P("batch", "seq", None)),
        check_vma=False,
    )
```

```python
import math

import jax
import jax.numpy as jnp
from jax import lax
from jax.experimental import pallas as pl
from jax.experimental.pallas import tpu as pltpu
from jax.sharding import PartitionSpec as P

C = 768
HEADS = 8
KSIZE = 5
LAYERS = 4
POOL = 16
PCH = 64
R = 8
ROWS = 384
GROUP = 4
LANES = 128
CT = C // LANES
REACH = 16
EDGE = LAYERS * REACH
SEG = ROWS // 8
STEP = 8
CHUNK = 128
PAIRS = HEADS // 2
WIN = 256
BF = jnp.bfloat16
F32 = jnp.float32
MESH = pl.DeviceIdType.MESH
ROOT = math.sqrt(2 / math.pi)
LOG2E = math.log2(math.e)


def gelu_of_double(half):
    u = half * (2 * ROOT + 8 * 0.044715 * ROOT * (half * half))
    return half + half * jnp.tanh(u)


def conv_stack(nat, seg, hbuf, taps_ref, dil_ref, low, high):
    def load(k, _):
        for j in range(8):
            q = k * 8 + j
            for c in range(CT):
                seg[c, q] = nat[c, pl.ds(q, 8, stride=SEG), :]
        return 0

    lax.fori_loop(0, SEG // 8, load, 0)

    def layer(l, _):
        d = dil_ref[l]

        for q in range(0, SEG, 8):
            rows = [seg[c, q : q + 8] for c in range(CT)]
            total = rows[0] * rows[0]
            for c in range(1, CT):
                total = total + rows[c] * rows[c]
            mean = jnp.sum(total, axis=-1, keepdims=True) * (1.0 / C)
            place = (
                lax.broadcasted_iota(jnp.int32, (8, 8, 1), 1) * SEG
                + lax.broadcasted_iota(jnp.int32, (8, 8, 1), 0)
                + q
            )
            scale = jnp.where((place >= low) & (place < high), lax.rsqrt(mean + 1e-06), 0.0)
            for c in range(CT):
                hbuf[c, q + REACH : q + REACH + 8] = rows[c] * scale
        for c in range(CT):
            hbuf[c, 0:REACH] = pltpu.roll(hbuf[c, SEG : SEG + REACH], 1, 1)
            hbuf[c, SEG + REACH : SEG + 2 * REACH] = pltpu.roll(
                hbuf[c, REACH : 2 * REACH], 7, 1
            )
        for c in range(CT):
            cols = slice(c * LANES, (c + 1) * LANES)
            taps = [
                jnp.broadcast_to(taps_ref[l, t : t + 1, cols], (8, LANES))[None]
                for t in range(KSIZE)
            ]

            for q in range(0, SEG, STEP):
                total = taps[0] * hbuf[c, pl.ds(q + REACH - 2 * d, STEP)]
                for t in range(1, KSIZE):
                    total = total + taps[t] * hbuf[c, pl.ds(q + REACH + (t - 2) * d, STEP)]
                seg[c, q : q + STEP] = seg[c, q : q + STEP] + gelu_of_double(total)
        return 0

    lax.fori_loop(0, LAYERS, layer, 0)

    def store(k, _):
        for j in range(8):
            q = k * 8 + j
            for c in range(CT):
                nat[c, pl.ds(q, 8, stride=SEG), :] = seg[c, q]
        return 0

    lax.fori_loop(0, SEG // 8, store, 0)


def kernel(
    x_ref, gain_ref, taps_ref, dil_ref, again_ref, wqkv_hbm, wout_hbm, wa_hbm, wb_hbm,
    track_ref, left_ref, rights,
    wqkv, wout, wa, wb, scaled, nat, seg, hbuf, state, halo, near, far, keys, values, q2,
    top, acc, mixed, wsem, send, recv,
):
    block = lax.axis_index("seq")
    core = lax.rem(block, 2)
    sibling = block + 1 - 2 * core
    partner = lax.rem(block + 2, GROUP)
    cross = GROUP - 1 - block

    def remote(src, dst, index, target):
        return pltpu.make_async_remote_copy(
            src_ref=src, dst_ref=dst, send_sem=send.at[index], recv_sem=recv.at[index],
            device_id={"seq": target}, device_id_type=MESH,
        )

    weights = [
        pltpu.make_async_copy(src, dst, wsem.at[i])
        for i, (src, dst) in enumerate(
            ((wqkv_hbm, wqkv), (wout_hbm, wout), (wa_hbm, wa), (wb_hbm, wb))
        )
    ]
    for copy in weights:
        copy.start()
    barrier = pltpu.get_barrier_semaphore()
    for target in (sibling, partner, cross):
        pl.semaphore_signal(barrier, inc=1, device_id={"seq": target}, device_id_type=MESH)

    to_left = remote(x_ref.at[pl.ds(0, EDGE)], halo.at[1], 0, lax.rem(block + GROUP - 1, GROUP))
    to_right = remote(
        x_ref.at[pl.ds(ROWS - EDGE, EDGE)], halo.at[0], 1, lax.rem(block + 1, GROUP)
    )
    has_left, has_right = block > 0, block < GROUP - 1

    upper = block >= GROUP // 2

    def meet():
        pl.semaphore_wait(barrier, 3)

        @pl.when(has_left)
        def _():
            to_left.start()

        @pl.when(has_right)
        def _():
            to_right.start()

    @pl.when(upper)
    def _():
        meet()

    for t in range(KSIZE):
        product = (taps_ref[t] * gain_ref[...]) * 0.5
        for l in range(LAYERS):
            scaled[l, t : t + 1] = product[l : l + 1]
    for c in range(CT):
        nat[c] = x_ref[:, c * LANES : (c + 1) * LANES].astype(F32)
    conv_stack(nat, seg, hbuf, scaled, dil_ref, 0, ROWS)

    def finish(source, target, count):
        rows = [nat[c, source : source + count] for c in range(CT)]
        total = rows[0] * rows[0]
        for c in range(1, CT):
            total = total + rows[c] * rows[c]
        scale = lax.rsqrt(jnp.sum(total, axis=-1, keepdims=True) * (1.0 / C) + 1e-06)
        for c in range(CT):
            cols = slice(c * LANES, (c + 1) * LANES)
            state[c, target : target + count] = rows[c]
            near[0, target : target + count, cols] = (
                rows[c] * scale * again_ref[cols][None]
            ).astype(BF)

    for start in range(EDGE, EDGE + CHUNK, 64):
        finish(start, start, 64)

    @pl.when(jnp.logical_not(upper))
    def _():
        meet()

    inner = [
        remote(
            near.at[0, pl.ds(EDGE + i * CHUNK, CHUNK)], far.at[0, pl.ds(i * CHUNK, CHUNK)],
            2 + i, partner,
        )
        for i in range(2)
    ]
    inner[0].start()
    for start in range(EDGE + CHUNK, ROWS - EDGE, 64):
        finish(start, start, 64)
    inner[1].start()
    inner_near = remote(
        near.at[0, pl.ds(EDGE, 2 * CHUNK)], near.at[1, pl.ds(EDGE, 2 * CHUNK)], 6, sibling
    )
    inner_near.start()

    @pl.when(has_left)
    def _():
        to_right.wait_recv()

    @pl.when(jnp.logical_not(has_left))
    def _():
        halo[0] = jnp.zeros((EDGE, C), BF)

    @pl.when(has_right)
    def _():
        to_left.wait_recv()

    @pl.when(jnp.logical_not(has_right))
    def _():
        halo[1] = jnp.zeros((EDGE, C), BF)

    for c in range(CT):
        cols = slice(c * LANES, (c + 1) * LANES)
        nat[c, 0:EDGE] = halo[0, :, cols].astype(F32)
        nat[c, EDGE : 3 * EDGE] = x_ref[0 : 2 * EDGE, cols].astype(F32)
        nat[c, 3 * EDGE : 5 * EDGE] = x_ref[ROWS - 2 * EDGE :, cols].astype(F32)
        nat[c, 5 * EDGE :] = halo[1, :, cols].astype(F32)
    conv_stack(
        nat, seg, hbuf, scaled, dil_ref,
        jnp.where(has_left, 0, EDGE), jnp.where(has_right, ROWS, ROWS - EDGE),
    )
    finish(EDGE, 0, EDGE)
    finish(ROWS - 2 * EDGE, ROWS - EDGE, EDGE)
    outer = []
    for i, start in enumerate((0, ROWS - EDGE)):
        rows = pl.ds(start, EDGE)
        outer.append(
            remote(
                near.at[0, rows], far.at[0, pl.ds(2 * CHUNK + i * EDGE, EDGE)], 4 + i, partner
            )
        )
        outer.append(remote(near.at[0, rows], near.at[1, rows], 7 + i, sibling))
    for copy in outer:
        copy.start()

    weights[0].wait()

    lane = lax.broadcasted_iota(jnp.int32, (1, WIN), 1)

    def project(source, column):
        return jnp.dot(
            source, wqkv[:, column : column + WIN], preferred_element_type=F32
        ).astype(BF)

    def window(p):
        return (p // 2) * (3 * LANES) + (p % 2) * LANES

    for p in range(PAIRS):
        rows = project(near[0], window(p))
        first = (p % 2) * 64
        for i in range(2):
            mine = (lane >= first + 96 * i) & (lane < first + 96 * (i + 1))
            q2[p, i * ROWS : (i + 1) * ROWS] = jnp.where(mine, rows, jnp.zeros_like(rows))

    def spare(p):
        first = (p % 2) * 64
        return (lane < first) | (lane >= first + 192)

    def keys_values(source, place, count):
        for t in range(C // WIN):
            keys[place : place + count, t * WIN : (t + 1) * WIN] = project(source, C + t * WIN)
        for p in range(PAIRS):
            rows = project(source, 2 * C + window(p))
            values[p, place : place + count] = jnp.where(spare(p), jnp.ones_like(rows), rows)

    TILE = 256
    SCALE = LOG2E / math.sqrt(C // HEADS)

    def attend(place, count, fresh):
        for p in range(PAIRS):
            cols = slice(window(p), window(p) + WIN)
            for t in range(2 * ROWS // TILE):
                rows = slice(t * TILE, (t + 1) * TILE)
                scores = lax.dot_general(
                    q2[p, rows], keys[place : place + count, cols],
                    (((1,), (1,)), ((), ())), preferred_element_type=F32,
                )
                pieces = [scores[:, j : j + LANES] for j in range(0, count, LANES)]
                peak = pieces[0]
                for piece in pieces[1:]:
                    peak = jnp.maximum(peak, piece)
                peak = jnp.broadcast_to(jnp.max(peak, axis=-1, keepdims=True), (TILE, LANES))
                if not fresh:
                    old = top[p, rows]
                    peak = jnp.maximum(peak, old)
                top[p, rows] = peak
                probs = jnp.concatenate(
                    [jnp.exp2((piece - peak) * SCALE).astype(BF) for piece in pieces], axis=1
                )
                out = jnp.dot(
                    probs, values[p, place : place + count], preferred_element_type=F32
                )
                if fresh:
                    acc[p, rows] = out
                else:
                    rescale = jnp.exp2((old - peak) * SCALE)
                    for j in range(0, WIN, LANES):
                        acc[p, rows, j : j + LANES] = (
                            acc[p, rows, j : j + LANES] * rescale + out[:, j : j + LANES]
                        )

    inner_near.wait_recv()
    outer[1].wait_recv()
    outer[3].wait_recv()
    keys_values(near[...].reshape(2 * ROWS, C), 0, 2 * ROWS)
    attend(0, 2 * ROWS, True)

    passes = []

    def pass_on(first, count, index):
        rows = pl.ds(first, count)
        onward = remote(far.at[0, rows], far.at[1, rows], index, sibling)
        onward.start()
        passes.append(onward)
        return onward

    inner[0].wait_recv()
    pass_on(0, CHUNK, 9).wait_recv()
    keys_values(far[:, :CHUNK].reshape(2 * CHUNK, C), 2 * ROWS, 2 * CHUNK)
    attend(2 * ROWS, 2 * CHUNK, False)
    inner[1].wait_recv()
    second = pass_on(CHUNK, CHUNK, 10)
    outer[0].wait_recv()
    third = pass_on(2 * CHUNK, EDGE, 11)
    second.wait_recv()
    third.wait_recv()
    count = CHUNK + EDGE
    place = 2 * ROWS + 2 * CHUNK
    keys_values(far[:, CHUNK : CHUNK + count].reshape(2 * count, C), place, 2 * count)
    attend(place, 2 * count, False)
    place = place + 2 * count
    outer[2].wait_recv()
    last = pass_on(ROWS - EDGE, EDGE, 12)
    keys_values(far[0, ROWS - EDGE :], place, EDGE)
    last.wait_recv()
    keys_values(far[1, ROWS - EDGE :], place + EDGE, EDGE)

    for g in range(2):
        parts = []
        for j in range(2):
            p = 2 * g + j
            cols = slice(window(p), window(p) + WIN)
            means = []
            for i in range(2):
                rows = slice(i * ROWS, (i + 1) * ROWS)
                scores = lax.dot_general(
                    q2[p, rows], keys[place:, cols],
                    (((1,), (1,)), ((), ())), preferred_element_type=F32,
                )
                old = top[p, rows]
                peak = jnp.maximum(old, jnp.max(scores, axis=-1, keepdims=True))
                probs = jnp.exp2((scores - peak) * SCALE).astype(BF)
                rescale = jnp.exp2((old - peak) * SCALE)
                out = jnp.dot(probs, values[p, place:], preferred_element_type=F32)
                total = [
                    acc[p, rows, k : k + LANES] * rescale + out[:, k : k + LANES]
                    for k in range(0, WIN, LANES)
                ]
                ones = total[1][:, 64:65] if j == 0 else total[0][:, 0:1]
                weight = 1.0 / ones
                means.append(jnp.concatenate([half * weight for half in total], axis=1))
            first = j * 64
            one = (lane >= first) & (lane < first + 96)
            two = (lane >= first + 96) & (lane < first + 192)
            parts.append(jnp.where(one, means[0], jnp.where(two, means[1], 0.0)))
        base = g * 3 * LANES
        mixed[:, base : base + LANES] = parts[0][:, :LANES].astype(BF)
        mixed[:, base + LANES : base + 2 * LANES] = (
            parts[0][:, LANES:] + parts[1][:, :LANES]
        ).astype(BF)
        mixed[:, base + 2 * LANES : base + 3 * LANES] = parts[1][:, LANES:].astype(BF)

    weights[1].wait()
    squares = jnp.zeros((ROWS // POOL, LANES), F32)
    pools = []
    for t in range(C // WIN):
        product = jnp.dot(
            mixed[...], wout[:, t * WIN : (t + 1) * WIN], preferred_element_type=F32
        )
        for j in range(WIN // LANES):
            c = t * (WIN // LANES) + j
            result = state[c] + product[:, j * LANES : (j + 1) * LANES]
            track_ref[:, c * LANES : (c + 1) * LANES] = result.astype(BF)
            pool = jnp.sum(result.reshape(ROWS // POOL, POOL, LANES), axis=1) * (1.0 / POOL)
            squares = squares + pool * pool
            pools.append(pool)
    scale = lax.rsqrt(jnp.sum(squares, axis=-1, keepdims=True) * (1.0 / C) + 1e-06)
    pooled = jnp.concatenate([pool * scale for pool in pools], axis=1).astype(BF)
    weights[3].wait()
    right = jnp.dot(pooled, wb[...], preferred_element_type=F32).astype(BF)
    rights[pl.ds(block, 1)] = right[None]
    shares = [
        remote(rights.at[block], rights.at[block], 13 + i, target)
        for i, target in enumerate((sibling, partner, cross))
    ]
    for copy in shares[::-1]:
        copy.start()
    weights[2].wait()
    left_ref[...] = jnp.dot(pooled, wa[...], preferred_element_type=F32).astype(BF)
    for copy in shares:
        copy.wait_recv()
    @pl.when(has_left)
    def _():
        to_left.wait_send()

    @pl.when(has_right)
    def _():
        to_right.wait_send()

    for copy in inner + [inner_near] + outer + passes + shares:
        copy.wait_send()


def finale(track_ref, left_ref, rights_ref, track_out, pair_ref, sem):
    copy = pltpu.make_async_copy(track_ref, track_out, sem)
    copy.start()
    left = left_ref[...].astype(F32)
    channel = lax.rem(lax.broadcasted_iota(jnp.int32, (PCH, 1, R * PCH), 2), PCH)
    wanted = lax.broadcasted_iota(jnp.int32, (PCH, 1, R * PCH), 0)
    spread = jnp.where(channel == wanted, left[None], 0.0)
    spread = spread.reshape(PCH * (ROWS // POOL), R * PCH).astype(BF)
    every = jnp.concatenate([rights_ref[i].astype(F32) for i in range(GROUP)], axis=0).astype(BF)
    product = lax.dot_general(
        spread, every, (((1,), (1,)), ((), ())), preferred_element_type=F32
    )
    pair_ref[...] = (
        (product * (1.0 / math.sqrt(R))).reshape(PCH, ROWS // POOL, GROUP * ROWS // POOL)
    ).astype(BF)
    copy.wait()


def body(x, conv_gain, conv_kernel, dilation, attn_gain, w_qkv, w_out, w_pair_a, w_pair_b):
    vmem = pl.BlockSpec(memory_space=pltpu.VMEM)
    hbm = pl.BlockSpec(memory_space=pl.ANY)
    track, left, rights = pl.pallas_call(
        kernel,
        out_shape=(
            pltpu.VMEM((ROWS, C), BF),
            pltpu.VMEM((ROWS // POOL, R * PCH), BF),
            pltpu.VMEM((GROUP, ROWS // POOL, R * PCH), BF),
        ),
        in_specs=[vmem, vmem, vmem, pl.BlockSpec(memory_space=pltpu.SMEM), vmem, hbm, hbm, hbm, hbm],
        out_specs=(vmem, vmem, vmem),
        scratch_shapes=[
            pltpu.VMEM(w_qkv.shape, BF),
            pltpu.VMEM(w_out.shape, BF),
            pltpu.VMEM(w_pair_a.shape, BF),
            pltpu.VMEM(w_pair_b.shape, BF),
            pltpu.VMEM((LAYERS, KSIZE, C), F32),
            pltpu.VMEM((CT, ROWS, LANES), F32),
            pltpu.VMEM((CT, SEG, 8, LANES), F32),
            pltpu.VMEM((CT, SEG + 2 * REACH, 8, LANES), F32),
            pltpu.VMEM((CT, ROWS, LANES), F32),
            pltpu.VMEM((2, EDGE, C), BF),
            pltpu.VMEM((2, ROWS, C), BF),
            pltpu.VMEM((2, ROWS, C), BF),
            pltpu.VMEM((GROUP * ROWS, C), BF),
            pltpu.VMEM((PAIRS, GROUP * ROWS, WIN), BF),
            pltpu.VMEM((PAIRS, 2 * ROWS, WIN), BF),
            pltpu.VMEM((PAIRS, 2 * ROWS, LANES), F32),
            pltpu.VMEM((PAIRS, 2 * ROWS, WIN), F32),
            pltpu.VMEM((ROWS, C), BF),
            pltpu.SemaphoreType.DMA((4,)),
            pltpu.SemaphoreType.DMA((16,)),
            pltpu.SemaphoreType.DMA((16,)),
        ],
        compiler_params=pltpu.CompilerParams(
            collective_id=0, has_side_effects=True, vmem_limit_bytes=60 * 1024 * 1024
        ),
    )(x, conv_gain, conv_kernel.transpose(1, 0, 2), dilation, attn_gain, w_qkv, w_out, w_pair_a, w_pair_b)
    return pl.pallas_call(
        finale,
        out_shape=(
            jax.ShapeDtypeStruct((ROWS, C), BF),
            jax.ShapeDtypeStruct((PCH, ROWS // POOL, GROUP * ROWS // POOL), BF),
        ),
        in_specs=[vmem, vmem, vmem],
        out_specs=(hbm, vmem),
        scratch_shapes=[pltpu.SemaphoreType.DMA],
    )(*[pltpu.with_memory_space_constraint(v, pltpu.VMEM) for v in (track, left, rights)])


def solution(mesh):
    placed = (P(("batch", "seq"), None), P(), P(), P(), P(), P(), P(), P(), P())
    return jax.shard_map(
        body,
        mesh=mesh,
        in_specs=placed,
        out_specs=(P(("batch", "seq"), None), P("batch", "seq", None)),
        check_vma=False,
    )
```

```python
import math

import jax
import jax.numpy as jnp
from jax import lax
from jax.experimental import pallas as pl
from jax.experimental.pallas import tpu as pltpu
from jax.sharding import PartitionSpec as P

C = 768
HEADS = 8
KSIZE = 5
LAYERS = 4
POOL = 16
PCH = 64
R = 8
ROWS = 384
GROUP = 4
LANES = 128
CT = C // LANES
REACH = 16
EDGE = LAYERS * REACH
SEG = ROWS // 8
STEP = 8
CHUNK = 128
PAIRS = HEADS // 2
WIN = 256
BF = jnp.bfloat16
F32 = jnp.float32
MESH = pl.DeviceIdType.MESH
ROOT = math.sqrt(2 / math.pi)
LOG2E = math.log2(math.e)


def gelu_of_double(half):
    u = half * (2 * ROOT + 8 * 0.044715 * ROOT * (half * half))
    return half + half * jnp.tanh(u)


def conv_stack(nat, seg, hbuf, taps_ref, dil_ref, low, high):
    def load(k, _):
        for j in range(8):
            q = k * 8 + j
            for c in range(CT):
                seg[c, q] = nat[c, pl.ds(q, 8, stride=SEG), :]
        return 0

    lax.fori_loop(0, SEG // 8, load, 0)

    def layer(l, _):
        d = dil_ref[l]

        for q in range(0, SEG, 8):
            rows = [seg[c, q : q + 8] for c in range(CT)]
            total = rows[0] * rows[0]
            for c in range(1, CT):
                total = total + rows[c] * rows[c]
            mean = jnp.sum(total, axis=-1, keepdims=True) * (1.0 / C)
            place = (
                lax.broadcasted_iota(jnp.int32, (8, 8, 1), 1) * SEG
                + lax.broadcasted_iota(jnp.int32, (8, 8, 1), 0)
                + q
            )
            scale = jnp.where((place >= low) & (place < high), lax.rsqrt(mean + 1e-06), 0.0)
            for c in range(CT):
                hbuf[c, q + REACH : q + REACH + 8] = rows[c] * scale
        for c in range(CT):
            hbuf[c, 0:REACH] = pltpu.roll(hbuf[c, SEG : SEG + REACH], 1, 1)
            hbuf[c, SEG + REACH : SEG + 2 * REACH] = pltpu.roll(
                hbuf[c, REACH : 2 * REACH], 7, 1
            )
        for c in range(CT):
            cols = slice(c * LANES, (c + 1) * LANES)
            taps = [
                jnp.broadcast_to(taps_ref[l, t : t + 1, cols], (8, LANES))[None]
                for t in range(KSIZE)
            ]

            for q in range(0, SEG, STEP):
                total = taps[0] * hbuf[c, pl.ds(q + REACH - 2 * d, STEP)]
                for t in range(1, KSIZE):
                    total = total + taps[t] * hbuf[c, pl.ds(q + REACH + (t - 2) * d, STEP)]
                seg[c, q : q + STEP] = seg[c, q : q + STEP] + gelu_of_double(total)
        return 0

    lax.fori_loop(0, LAYERS, layer, 0)

    def store(k, _):
        for j in range(8):
            q = k * 8 + j
            for c in range(CT):
                nat[c, pl.ds(q, 8, stride=SEG), :] = seg[c, q]
        return 0

    lax.fori_loop(0, SEG // 8, store, 0)


def kernel(
    x_ref, gain_ref, taps_ref, dil_ref, again_ref, wqkv_hbm, wout_hbm, wa_hbm, wb_hbm,
    track_ref, left_ref, rights,
    wqkv, wout, wa, wb, scaled, nat, seg, hbuf, state, halo, near, far, keys, values, q2,
    top, acc, mixed, wsem, send, recv,
):
    block = lax.axis_index("seq")
    core = lax.rem(block, 2)
    sibling = block + 1 - 2 * core
    partner = lax.rem(block + 2, GROUP)
    cross = GROUP - 1 - block

    def remote(src, dst, index, target):
        return pltpu.make_async_remote_copy(
            src_ref=src, dst_ref=dst, send_sem=send.at[index], recv_sem=recv.at[index],
            device_id={"seq": target}, device_id_type=MESH,
        )

    weights = [
        pltpu.make_async_copy(src, dst, wsem.at[i])
        for i, (src, dst) in enumerate(
            ((wqkv_hbm, wqkv), (wout_hbm, wout), (wa_hbm, wa), (wb_hbm, wb))
        )
    ]
    for copy in weights:
        copy.start()
    barrier = pltpu.get_barrier_semaphore()
    for target in (sibling, partner, cross):
        pl.semaphore_signal(barrier, inc=1, device_id={"seq": target}, device_id_type=MESH)

    to_left = remote(x_ref.at[pl.ds(0, EDGE)], halo.at[1], 0, lax.rem(block + GROUP - 1, GROUP))
    to_right = remote(
        x_ref.at[pl.ds(ROWS - EDGE, EDGE)], halo.at[0], 1, lax.rem(block + 1, GROUP)
    )
    has_left, has_right = block > 0, block < GROUP - 1

    upper = block >= GROUP // 2

    def meet():
        pl.semaphore_wait(barrier, 3)

        @pl.when(has_left)
        def _():
            to_left.start()

        @pl.when(has_right)
        def _():
            to_right.start()

    @pl.when(upper)
    def _():
        meet()

    for t in range(KSIZE):
        product = (taps_ref[t] * gain_ref[...]) * 0.5
        for l in range(LAYERS):
            scaled[l, t : t + 1] = product[l : l + 1]
    for c in range(CT):
        nat[c] = x_ref[:, c * LANES : (c + 1) * LANES].astype(F32)
    conv_stack(nat, seg, hbuf, scaled, dil_ref, 0, ROWS)

    def finish(source, target, count):
        rows = [nat[c, source : source + count] for c in range(CT)]
        total = rows[0] * rows[0]
        for c in range(1, CT):
            total = total + rows[c] * rows[c]
        scale = lax.rsqrt(jnp.sum(total, axis=-1, keepdims=True) * (1.0 / C) + 1e-06)
        for c in range(CT):
            cols = slice(c * LANES, (c + 1) * LANES)
            state[c, target : target + count] = rows[c]
            near[0, target : target + count, cols] = (
                rows[c] * scale * again_ref[cols][None]
            ).astype(BF)

    for start in range(EDGE, EDGE + CHUNK, 64):
        finish(start, start, 64)

    @pl.when(jnp.logical_not(upper))
    def _():
        meet()

    inner = [
        remote(
            near.at[0, pl.ds(EDGE + i * CHUNK, CHUNK)], far.at[0, pl.ds(i * CHUNK, CHUNK)],
            2 + i, partner,
        )
        for i in range(2)
    ]
    inner[0].start()
    for start in range(EDGE + CHUNK, ROWS - EDGE, 64):
        finish(start, start, 64)
    inner[1].start()
    inner_near = remote(
        near.at[0, pl.ds(EDGE, 2 * CHUNK)], near.at[1, pl.ds(EDGE, 2 * CHUNK)], 6, sibling
    )
    inner_near.start()

    @pl.when(has_left)
    def _():
        to_right.wait_recv()

    @pl.when(jnp.logical_not(has_left))
    def _():
        halo[0] = jnp.zeros((EDGE, C), BF)

    @pl.when(has_right)
    def _():
        to_left.wait_recv()

    @pl.when(jnp.logical_not(has_right))
    def _():
        halo[1] = jnp.zeros((EDGE, C), BF)

    for c in range(CT):
        cols = slice(c * LANES, (c + 1) * LANES)
        nat[c, 0:EDGE] = halo[0, :, cols].astype(F32)
        nat[c, EDGE : 3 * EDGE] = x_ref[0 : 2 * EDGE, cols].astype(F32)
        nat[c, 3 * EDGE : 5 * EDGE] = x_ref[ROWS - 2 * EDGE :, cols].astype(F32)
        nat[c, 5 * EDGE :] = halo[1, :, cols].astype(F32)
    conv_stack(
        nat, seg, hbuf, scaled, dil_ref,
        jnp.where(has_left, 0, EDGE), jnp.where(has_right, ROWS, ROWS - EDGE),
    )
    finish(EDGE, 0, EDGE)
    finish(ROWS - 2 * EDGE, ROWS - EDGE, EDGE)
    outer = []
    for i, start in enumerate((0, ROWS - EDGE)):
        rows = pl.ds(start, EDGE)
        outer.append(
            remote(
                near.at[0, rows], far.at[0, pl.ds(2 * CHUNK + i * EDGE, EDGE)], 4 + i, partner
            )
        )
        outer.append(remote(near.at[0, rows], near.at[1, rows], 7 + i, sibling))
    for copy in outer:
        copy.start()

    weights[0].wait()

    lane = lax.broadcasted_iota(jnp.int32, (1, WIN), 1)

    def project(source, column):
        return jnp.dot(
            source, wqkv[:, column : column + WIN], preferred_element_type=F32
        ).astype(BF)

    def window(p):
        return (p // 2) * (3 * LANES) + (p % 2) * LANES

    for p in range(PAIRS):
        rows = project(near[0], window(p))
        first = (p % 2) * 64
        for i in range(2):
            mine = (lane >= first + 96 * i) & (lane < first + 96 * (i + 1))
            q2[p, i * ROWS : (i + 1) * ROWS] = jnp.where(mine, rows, jnp.zeros_like(rows))

    def spare(p):
        first = (p % 2) * 64
        return (lane < first) | (lane >= first + 192)

    def keys_values(source, place, count):
        for t in range(C // WIN):
            keys[place : place + count, t * WIN : (t + 1) * WIN] = project(source, C + t * WIN)
        for p in range(PAIRS):
            rows = project(source, 2 * C + window(p))
            values[p, place : place + count] = jnp.where(spare(p), jnp.ones_like(rows), rows)

    TILE = 256
    SCALE = LOG2E / math.sqrt(C // HEADS)

    def attend(place, count, fresh):
        for p in range(PAIRS):
            cols = slice(window(p), window(p) + WIN)
            for t in range(2 * ROWS // TILE):
                rows = slice(t * TILE, (t + 1) * TILE)
                scores = lax.dot_general(
                    q2[p, rows], keys[place : place + count, cols],
                    (((1,), (1,)), ((), ())), preferred_element_type=F32,
                )
                pieces = [scores[:, j : j + LANES] for j in range(0, count, LANES)]
                peak = pieces[0]
                for piece in pieces[1:]:
                    peak = jnp.maximum(peak, piece)
                peak = jnp.broadcast_to(jnp.max(peak, axis=-1, keepdims=True), (TILE, LANES))
                if not fresh:
                    old = top[p, rows]
                    peak = jnp.maximum(peak, old)
                top[p, rows] = peak
                probs = jnp.concatenate(
                    [jnp.exp2((piece - peak) * SCALE).astype(BF) for piece in pieces], axis=1
                )
                out = jnp.dot(
                    probs, values[p, place : place + count], preferred_element_type=F32
                )
                if fresh:
                    acc[p, rows] = out
                else:
                    rescale = jnp.exp2((old - peak) * SCALE)
                    for j in range(0, WIN, LANES):
                        acc[p, rows, j : j + LANES] = (
                            acc[p, rows, j : j + LANES] * rescale + out[:, j : j + LANES]
                        )

    inner_near.wait_recv()
    outer[1].wait_recv()
    outer[3].wait_recv()
    keys_values(near[...].reshape(2 * ROWS, C), 0, 2 * ROWS)
    attend(0, 2 * ROWS, True)

    passes = []

    def pass_on(first, count, index):
        rows = pl.ds(first, count)
        onward = remote(far.at[0, rows], far.at[1, rows], index, sibling)
        onward.start()
        passes.append(onward)
        return onward

    inner[0].wait_recv()
    pass_on(0, CHUNK, 9).wait_recv()
    keys_values(far[:, :CHUNK].reshape(2 * CHUNK, C), 2 * ROWS, 2 * CHUNK)
    attend(2 * ROWS, 2 * CHUNK, False)
    inner[1].wait_recv()
    pass_on(CHUNK, CHUNK, 10).wait_recv()
    keys_values(far[:, CHUNK : 2 * CHUNK].reshape(2 * CHUNK, C), 2 * ROWS + 2 * CHUNK, 2 * CHUNK)
    attend(2 * ROWS + 2 * CHUNK, 2 * CHUNK, False)
    place = 2 * ROWS + 4 * CHUNK
    outer[0].wait_recv()
    last = [pass_on(2 * CHUNK, EDGE, 11)]
    outer[2].wait_recv()
    last.append(pass_on(2 * CHUNK + EDGE, EDGE, 12))
    keys_values(far[0, 2 * CHUNK :], place, CHUNK)
    for copy in last:
        copy.wait_recv()
    keys_values(far[1, 2 * CHUNK :], place + CHUNK, CHUNK)

    for g in range(2):
        parts = []
        for j in range(2):
            p = 2 * g + j
            cols = slice(window(p), window(p) + WIN)
            means = []
            for i in range(2):
                rows = slice(i * ROWS, (i + 1) * ROWS)
                scores = lax.dot_general(
                    q2[p, rows], keys[place:, cols],
                    (((1,), (1,)), ((), ())), preferred_element_type=F32,
                )
                old = top[p, rows]
                pieces = [scores[:, k : k + LANES] for k in range(0, 2 * CHUNK, LANES)]
                peak = jnp.max(jnp.maximum(*pieces), axis=-1, keepdims=True)
                peak = jnp.maximum(old, peak)
                probs = jnp.concatenate(
                    [jnp.exp2((piece - peak) * SCALE).astype(BF) for piece in pieces], axis=1
                )
                rescale = jnp.exp2((old - peak) * SCALE)
                out = jnp.dot(probs, values[p, place:], preferred_element_type=F32)
                total = [
                    acc[p, rows, k : k + LANES] * rescale + out[:, k : k + LANES]
                    for k in range(0, WIN, LANES)
                ]
                ones = total[1][:, 64:65] if j == 0 else total[0][:, 0:1]
                weight = 1.0 / ones
                means.append(jnp.concatenate([half * weight for half in total], axis=1))
            first = j * 64
            one = (lane >= first) & (lane < first + 96)
            two = (lane >= first + 96) & (lane < first + 192)
            parts.append(jnp.where(one, means[0], jnp.where(two, means[1], 0.0)))
        base = g * 3 * LANES
        mixed[:, base : base + LANES] = parts[0][:, :LANES].astype(BF)
        mixed[:, base + LANES : base + 2 * LANES] = (
            parts[0][:, LANES:] + parts[1][:, :LANES]
        ).astype(BF)
        mixed[:, base + 2 * LANES : base + 3 * LANES] = parts[1][:, LANES:].astype(BF)

    weights[1].wait()
    squares = jnp.zeros((ROWS // POOL, LANES), F32)
    pools = []
    for t in range(C // WIN):
        product = jnp.dot(
            mixed[...], wout[:, t * WIN : (t + 1) * WIN], preferred_element_type=F32
        )
        for j in range(WIN // LANES):
            c = t * (WIN // LANES) + j
            result = state[c] + product[:, j * LANES : (j + 1) * LANES]
            track_ref[:, c * LANES : (c + 1) * LANES] = result.astype(BF)
            pool = jnp.sum(result.reshape(ROWS // POOL, POOL, LANES), axis=1) * (1.0 / POOL)
            squares = squares + pool * pool
            pools.append(pool)
    scale = lax.rsqrt(jnp.sum(squares, axis=-1, keepdims=True) * (1.0 / C) + 1e-06)
    pooled = jnp.concatenate([pool * scale for pool in pools], axis=1).astype(BF)
    weights[3].wait()
    right = jnp.dot(pooled, wb[...], preferred_element_type=F32).astype(BF)
    rights[pl.ds(block, 1)] = right[None]
    shares = [
        remote(rights.at[block], rights.at[block], 13 + i, target)
        for i, target in enumerate((sibling, partner, cross))
    ]
    for copy in shares[::-1]:
        copy.start()
    weights[2].wait()
    left_ref[...] = jnp.dot(pooled, wa[...], preferred_element_type=F32).astype(BF)
    for copy in shares:
        copy.wait_recv()
    @pl.when(has_left)
    def _():
        to_left.wait_send()

    @pl.when(has_right)
    def _():
        to_right.wait_send()

    for copy in inner + [inner_near] + outer + passes + shares:
        copy.wait_send()


def finale(track_ref, left_ref, rights_ref, track_out, pair_ref, sem):
    copy = pltpu.make_async_copy(track_ref, track_out, sem)
    copy.start()
    left = left_ref[...].astype(F32)
    channel = lax.rem(lax.broadcasted_iota(jnp.int32, (PCH, 1, R * PCH), 2), PCH)
    wanted = lax.broadcasted_iota(jnp.int32, (PCH, 1, R * PCH), 0)
    spread = jnp.where(channel == wanted, left[None], 0.0)
    spread = spread.reshape(PCH * (ROWS // POOL), R * PCH).astype(BF)
    every = jnp.concatenate([rights_ref[i].astype(F32) for i in range(GROUP)], axis=0).astype(BF)
    product = lax.dot_general(
        spread, every, (((1,), (1,)), ((), ())), preferred_element_type=F32
    )
    pair_ref[...] = (
        (product * (1.0 / math.sqrt(R))).reshape(PCH, ROWS // POOL, GROUP * ROWS // POOL)
    ).astype(BF)
    copy.wait()


def body(x, conv_gain, conv_kernel, dilation, attn_gain, w_qkv, w_out, w_pair_a, w_pair_b):
    vmem = pl.BlockSpec(memory_space=pltpu.VMEM)
    hbm = pl.BlockSpec(memory_space=pl.ANY)
    track, left, rights = pl.pallas_call(
        kernel,
        out_shape=(
            pltpu.VMEM((ROWS, C), BF),
            pltpu.VMEM((ROWS // POOL, R * PCH), BF),
            pltpu.VMEM((GROUP, ROWS // POOL, R * PCH), BF),
        ),
        in_specs=[vmem, vmem, vmem, pl.BlockSpec(memory_space=pltpu.SMEM), vmem, hbm, hbm, hbm, hbm],
        out_specs=(vmem, vmem, vmem),
        scratch_shapes=[
            pltpu.VMEM(w_qkv.shape, BF),
            pltpu.VMEM(w_out.shape, BF),
            pltpu.VMEM(w_pair_a.shape, BF),
            pltpu.VMEM(w_pair_b.shape, BF),
            pltpu.VMEM((LAYERS, KSIZE, C), F32),
            pltpu.VMEM((CT, ROWS, LANES), F32),
            pltpu.VMEM((CT, SEG, 8, LANES), F32),
            pltpu.VMEM((CT, SEG + 2 * REACH, 8, LANES), F32),
            pltpu.VMEM((CT, ROWS, LANES), F32),
            pltpu.VMEM((2, EDGE, C), BF),
            pltpu.VMEM((2, ROWS, C), BF),
            pltpu.VMEM((2, ROWS, C), BF),
            pltpu.VMEM((GROUP * ROWS, C), BF),
            pltpu.VMEM((PAIRS, GROUP * ROWS, WIN), BF),
            pltpu.VMEM((PAIRS, 2 * ROWS, WIN), BF),
            pltpu.VMEM((PAIRS, 2 * ROWS, LANES), F32),
            pltpu.VMEM((PAIRS, 2 * ROWS, WIN), F32),
            pltpu.VMEM((ROWS, C), BF),
            pltpu.SemaphoreType.DMA((4,)),
            pltpu.SemaphoreType.DMA((16,)),
            pltpu.SemaphoreType.DMA((16,)),
        ],
        compiler_params=pltpu.CompilerParams(
            collective_id=0, has_side_effects=True, vmem_limit_bytes=60 * 1024 * 1024
        ),
    )(x, conv_gain, conv_kernel.transpose(1, 0, 2), dilation, attn_gain, w_qkv, w_out, w_pair_a, w_pair_b)
    return pl.pallas_call(
        finale,
        out_shape=(
            jax.ShapeDtypeStruct((ROWS, C), BF),
            jax.ShapeDtypeStruct((PCH, ROWS // POOL, GROUP * ROWS // POOL), BF),
        ),
        in_specs=[vmem, vmem, vmem],
        out_specs=(hbm, vmem),
        scratch_shapes=[pltpu.SemaphoreType.DMA],
    )(*[pltpu.with_memory_space_constraint(v, pltpu.VMEM) for v in (track, left, rights)])


def solution(mesh):
    placed = (P(("batch", "seq"), None), P(), P(), P(), P(), P(), P(), P(), P())
    return jax.shard_map(
        body,
        mesh=mesh,
        in_specs=placed,
        out_specs=(P(("batch", "seq"), None), P("batch", "seq", None)),
        check_vma=False,
    )
```

```python
import math

import jax
import jax.numpy as jnp
from jax import lax
from jax.experimental import pallas as pl
from jax.experimental.pallas import tpu as pltpu
from jax.sharding import PartitionSpec as P

C = 768
HEADS = 8
KSIZE = 5
LAYERS = 4
POOL = 16
PCH = 64
R = 8
ROWS = 384
GROUP = 4
LANES = 128
CT = C // LANES
REACH = 16
EDGE = LAYERS * REACH
SEG = ROWS // 8
STEP = 8
CHUNK = 128
PAIRS = HEADS // 2
WIN = 256
BF = jnp.bfloat16
F32 = jnp.float32
MESH = pl.DeviceIdType.MESH
ROOT = math.sqrt(2 / math.pi)
LOG2E = math.log2(math.e)


def gelu_of_double(half):
    u = half * (2 * ROOT + 8 * 0.044715 * ROOT * (half * half))
    return half + half * jnp.tanh(u)


def conv_stack(nat, seg, hbuf, taps_ref, dil_ref, low, high):
    def load(k, _):
        for j in range(8):
            q = k * 8 + j
            for c in range(CT):
                seg[c, q] = nat[c, pl.ds(q, 8, stride=SEG), :]
        return 0

    lax.fori_loop(0, SEG // 8, load, 0)

    def layer(l, _):
        d = dil_ref[l]

        for q in range(0, SEG, 8):
            rows = [seg[c, q : q + 8] for c in range(CT)]
            total = rows[0] * rows[0]
            for c in range(1, CT):
                total = total + rows[c] * rows[c]
            mean = jnp.sum(total, axis=-1, keepdims=True) * (1.0 / C)
            place = (
                lax.broadcasted_iota(jnp.int32, (8, 8, 1), 1) * SEG
                + lax.broadcasted_iota(jnp.int32, (8, 8, 1), 0)
                + q
            )
            scale = jnp.where((place >= low) & (place < high), lax.rsqrt(mean + 1e-06), 0.0)
            for c in range(CT):
                hbuf[c, q + REACH : q + REACH + 8] = rows[c] * scale
        for c in range(CT):
            hbuf[c, 0:REACH] = pltpu.roll(hbuf[c, SEG : SEG + REACH], 1, 1)
            hbuf[c, SEG + REACH : SEG + 2 * REACH] = pltpu.roll(
                hbuf[c, REACH : 2 * REACH], 7, 1
            )
        for c in range(CT):
            cols = slice(c * LANES, (c + 1) * LANES)
            taps = [
                jnp.broadcast_to(taps_ref[l, t : t + 1, cols], (8, LANES))[None]
                for t in range(KSIZE)
            ]

            for q in range(0, SEG, STEP):
                total = taps[0] * hbuf[c, pl.ds(q + REACH - 2 * d, STEP)]
                for t in range(1, KSIZE):
                    total = total + taps[t] * hbuf[c, pl.ds(q + REACH + (t - 2) * d, STEP)]
                seg[c, q : q + STEP] = seg[c, q : q + STEP] + gelu_of_double(total)
        return 0

    lax.fori_loop(0, LAYERS, layer, 0)

    def store(k, _):
        for j in range(8):
            q = k * 8 + j
            for c in range(CT):
                nat[c, pl.ds(q, 8, stride=SEG), :] = seg[c, q]
        return 0

    lax.fori_loop(0, SEG // 8, store, 0)


def kernel(
    x_ref, gain_ref, taps_ref, dil_ref, again_ref, wqkv_hbm, wout_hbm, wa_hbm, wb_hbm,
    track_ref, spread_ref, rights,
    wqkv, wout, wa, wb, scaled, nat, seg, hbuf, state, halo, near, far, keys, values, q2,
    top, acc, mixed, wsem, send, recv,
):
    block = lax.axis_index("seq")
    core = lax.rem(block, 2)
    sibling = block + 1 - 2 * core
    partner = lax.rem(block + 2, GROUP)
    cross = GROUP - 1 - block

    def remote(src, dst, index, target):
        return pltpu.make_async_remote_copy(
            src_ref=src, dst_ref=dst, send_sem=send.at[index], recv_sem=recv.at[index],
            device_id={"seq": target}, device_id_type=MESH,
        )

    weights = [
        pltpu.make_async_copy(src, dst, wsem.at[i])
        for i, (src, dst) in enumerate(
            ((wqkv_hbm, wqkv), (wout_hbm, wout), (wa_hbm, wa), (wb_hbm, wb))
        )
    ]
    for copy in weights:
        copy.start()
    barrier = pltpu.get_barrier_semaphore()
    for target in (sibling, partner, cross):
        pl.semaphore_signal(barrier, inc=1, device_id={"seq": target}, device_id_type=MESH)

    to_left = remote(x_ref.at[pl.ds(0, EDGE)], halo.at[1], 0, lax.rem(block + GROUP - 1, GROUP))
    to_right = remote(
        x_ref.at[pl.ds(ROWS - EDGE, EDGE)], halo.at[0], 1, lax.rem(block + 1, GROUP)
    )
    has_left, has_right = block > 0, block < GROUP - 1

    upper = block >= GROUP // 2

    def meet():
        pl.semaphore_wait(barrier, 3)

        @pl.when(has_left)
        def _():
            to_left.start()

        @pl.when(has_right)
        def _():
            to_right.start()

    @pl.when(upper)
    def _():
        meet()

    for t in range(KSIZE):
        product = (taps_ref[t] * gain_ref[...]) * 0.5
        for l in range(LAYERS):
            scaled[l, t : t + 1] = product[l : l + 1]
    for c in range(CT):
        nat[c] = x_ref[:, c * LANES : (c + 1) * LANES].astype(F32)
    conv_stack(nat, seg, hbuf, scaled, dil_ref, 0, ROWS)

    def finish(source, target, count):
        rows = [nat[c, source : source + count] for c in range(CT)]
        total = rows[0] * rows[0]
        for c in range(1, CT):
            total = total + rows[c] * rows[c]
        scale = lax.rsqrt(jnp.sum(total, axis=-1, keepdims=True) * (1.0 / C) + 1e-06)
        for c in range(CT):
            cols = slice(c * LANES, (c + 1) * LANES)
            state[c, target : target + count] = rows[c]
            near[0, target : target + count, cols] = (
                rows[c] * scale * again_ref[cols][None]
            ).astype(BF)

    for start in range(EDGE, EDGE + CHUNK, 64):
        finish(start, start, 64)

    @pl.when(jnp.logical_not(upper))
    def _():
        meet()

    inner = [
        remote(
            near.at[0, pl.ds(EDGE + i * CHUNK, CHUNK)], far.at[0, pl.ds(i * CHUNK, CHUNK)],
            2 + i, partner,
        )
        for i in range(2)
    ]
    inner[0].start()
    for start in range(EDGE + CHUNK, ROWS - EDGE, 64):
        finish(start, start, 64)
    inner[1].start()
    inner_near = remote(
        near.at[0, pl.ds(EDGE, 2 * CHUNK)], near.at[1, pl.ds(EDGE, 2 * CHUNK)], 6, sibling
    )
    inner_near.start()

    @pl.when(has_left)
    def _():
        to_right.wait_recv()

    @pl.when(jnp.logical_not(has_left))
    def _():
        halo[0] = jnp.zeros((EDGE, C), BF)

    @pl.when(has_right)
    def _():
        to_left.wait_recv()

    @pl.when(jnp.logical_not(has_right))
    def _():
        halo[1] = jnp.zeros((EDGE, C), BF)

    for c in range(CT):
        cols = slice(c * LANES, (c + 1) * LANES)
        nat[c, 0:EDGE] = halo[0, :, cols].astype(F32)
        nat[c, EDGE : 3 * EDGE] = x_ref[0 : 2 * EDGE, cols].astype(F32)
        nat[c, 3 * EDGE : 5 * EDGE] = x_ref[ROWS - 2 * EDGE :, cols].astype(F32)
        nat[c, 5 * EDGE :] = halo[1, :, cols].astype(F32)
    conv_stack(
        nat, seg, hbuf, scaled, dil_ref,
        jnp.where(has_left, 0, EDGE), jnp.where(has_right, ROWS, ROWS - EDGE),
    )
    finish(EDGE, 0, EDGE)
    finish(ROWS - 2 * EDGE, ROWS - EDGE, EDGE)
    outer = []
    for i, start in enumerate((0, ROWS - EDGE)):
        rows = pl.ds(start, EDGE)
        outer.append(
            remote(
                near.at[0, rows], far.at[0, pl.ds(2 * CHUNK + i * EDGE, EDGE)], 4 + i, partner
            )
        )
        outer.append(remote(near.at[0, rows], near.at[1, rows], 7 + i, sibling))
    for copy in outer:
        copy.start()

    weights[0].wait()

    lane = lax.broadcasted_iota(jnp.int32, (1, WIN), 1)

    def project(source, column):
        return jnp.dot(
            source, wqkv[:, column : column + WIN], preferred_element_type=F32
        ).astype(BF)

    def window(p):
        return (p // 2) * (3 * LANES) + (p % 2) * LANES

    for p in range(PAIRS):
        rows = project(near[0], window(p))
        first = (p % 2) * 64
        for i in range(2):
            mine = (lane >= first + 96 * i) & (lane < first + 96 * (i + 1))
            q2[p, i * ROWS : (i + 1) * ROWS] = jnp.where(mine, rows, jnp.zeros_like(rows))

    def spare(p):
        first = (p % 2) * 64
        return (lane < first) | (lane >= first + 192)

    def keys_values(source, place, count):
        for t in range(C // WIN):
            keys[place : place + count, t * WIN : (t + 1) * WIN] = project(source, C + t * WIN)
        for p in range(PAIRS):
            rows = project(source, 2 * C + window(p))
            values[p, place : place + count] = jnp.where(spare(p), jnp.ones_like(rows), rows)

    TILE = 256
    SCALE = LOG2E / math.sqrt(C // HEADS)

    def attend(place, count, fresh):
        for p in range(PAIRS):
            cols = slice(window(p), window(p) + WIN)
            for t in range(2 * ROWS // TILE):
                rows = slice(t * TILE, (t + 1) * TILE)
                scores = lax.dot_general(
                    q2[p, rows], keys[place : place + count, cols],
                    (((1,), (1,)), ((), ())), preferred_element_type=F32,
                )
                pieces = [scores[:, j : j + LANES] for j in range(0, count, LANES)]
                peak = pieces[0]
                for piece in pieces[1:]:
                    peak = jnp.maximum(peak, piece)
                peak = jnp.broadcast_to(jnp.max(peak, axis=-1, keepdims=True), (TILE, LANES))
                if not fresh:
                    old = top[p, rows]
                    peak = jnp.maximum(peak, old)
                top[p, rows] = peak
                probs = jnp.concatenate(
                    [jnp.exp2((piece - peak) * SCALE).astype(BF) for piece in pieces], axis=1
                )
                out = jnp.dot(
                    probs, values[p, place : place + count], preferred_element_type=F32
                )
                if fresh:
                    acc[p, rows] = out
                else:
                    rescale = jnp.exp2((old - peak) * SCALE)
                    for j in range(0, WIN, LANES):
                        acc[p, rows, j : j + LANES] = (
                            acc[p, rows, j : j + LANES] * rescale + out[:, j : j + LANES]
                        )

    inner_near.wait_recv()
    outer[1].wait_recv()
    outer[3].wait_recv()
    keys_values(near[...].reshape(2 * ROWS, C), 0, 2 * ROWS)
    attend(0, 2 * ROWS, True)

    passes = []

    def pass_on(first, count, index):
        rows = pl.ds(first, count)
        onward = remote(far.at[0, rows], far.at[1, rows], index, sibling)
        onward.start()
        passes.append(onward)
        return onward

    inner[0].wait_recv()
    pass_on(0, CHUNK, 9).wait_recv()
    keys_values(far[:, :CHUNK].reshape(2 * CHUNK, C), 2 * ROWS, 2 * CHUNK)
    attend(2 * ROWS, 2 * CHUNK, False)
    inner[1].wait_recv()
    pass_on(CHUNK, CHUNK, 10).wait_recv()
    keys_values(far[:, CHUNK : 2 * CHUNK].reshape(2 * CHUNK, C), 2 * ROWS + 2 * CHUNK, 2 * CHUNK)
    attend(2 * ROWS + 2 * CHUNK, 2 * CHUNK, False)
    place = 2 * ROWS + 4 * CHUNK
    outer[0].wait_recv()
    last = [pass_on(2 * CHUNK, EDGE, 11)]
    outer[2].wait_recv()
    last.append(pass_on(2 * CHUNK + EDGE, EDGE, 12))
    keys_values(far[0, 2 * CHUNK :], place, CHUNK)
    for copy in last:
        copy.wait_recv()
    keys_values(far[1, 2 * CHUNK :], place + CHUNK, CHUNK)

    for g in range(2):
        parts = []
        for j in range(2):
            p = 2 * g + j
            cols = slice(window(p), window(p) + WIN)
            means = []
            for i in range(2):
                rows = slice(i * ROWS, (i + 1) * ROWS)
                scores = lax.dot_general(
                    q2[p, rows], keys[place:, cols],
                    (((1,), (1,)), ((), ())), preferred_element_type=F32,
                )
                old = top[p, rows]
                pieces = [scores[:, k : k + LANES] for k in range(0, 2 * CHUNK, LANES)]
                peak = jnp.max(jnp.maximum(*pieces), axis=-1, keepdims=True)
                peak = jnp.maximum(old, peak)
                probs = jnp.concatenate(
                    [jnp.exp2((piece - peak) * SCALE).astype(BF) for piece in pieces], axis=1
                )
                rescale = jnp.exp2((old - peak) * SCALE)
                out = jnp.dot(probs, values[p, place:], preferred_element_type=F32)
                total = [
                    acc[p, rows, k : k + LANES] * rescale + out[:, k : k + LANES]
                    for k in range(0, WIN, LANES)
                ]
                ones = total[1][:, 64:65] if j == 0 else total[0][:, 0:1]
                weight = 1.0 / ones
                means.append(jnp.concatenate([half * weight for half in total], axis=1))
            first = j * 64
            one = (lane >= first) & (lane < first + 96)
            two = (lane >= first + 96) & (lane < first + 192)
            parts.append(jnp.where(one, means[0], jnp.where(two, means[1], 0.0)))
        base = g * 3 * LANES
        mixed[:, base : base + LANES] = parts[0][:, :LANES].astype(BF)
        mixed[:, base + LANES : base + 2 * LANES] = (
            parts[0][:, LANES:] + parts[1][:, :LANES]
        ).astype(BF)
        mixed[:, base + 2 * LANES : base + 3 * LANES] = parts[1][:, LANES:].astype(BF)

    weights[1].wait()
    squares = jnp.zeros((ROWS // POOL, LANES), F32)
    pools = []
    for t in range(C // WIN):
        product = jnp.dot(
            mixed[...], wout[:, t * WIN : (t + 1) * WIN], preferred_element_type=F32
        )
        for j in range(WIN // LANES):
            c = t * (WIN // LANES) + j
            result = state[c] + product[:, j * LANES : (j + 1) * LANES]
            state[c] = result
            pool = jnp.sum(result.reshape(ROWS // POOL, POOL, LANES), axis=1) * (1.0 / POOL)
            squares = squares + pool * pool
            pools.append(pool)
    scale = lax.rsqrt(jnp.sum(squares, axis=-1, keepdims=True) * (1.0 / C) + 1e-06)
    pooled = jnp.concatenate([pool * scale for pool in pools], axis=1).astype(BF)
    weights[3].wait()
    right = jnp.dot(pooled, wb[...], preferred_element_type=F32).astype(BF)
    rights[pl.ds(block, 1)] = right[None]
    shares = [
        remote(rights.at[block], rights.at[block], 13 + i, target)
        for i, target in enumerate((sibling, partner, cross))
    ]
    for copy in shares[::-1]:
        copy.start()
    for c in range(CT):
        track_ref[:, c * LANES : (c + 1) * LANES] = state[c].astype(BF)
    weights[2].wait()
    left = jnp.dot(pooled, wa[...], preferred_element_type=F32).astype(BF).astype(F32)
    channel = lax.rem(lax.broadcasted_iota(jnp.int32, (PCH, 1, R * PCH), 2), PCH)
    wanted = lax.broadcasted_iota(jnp.int32, (PCH, 1, R * PCH), 0)
    spread = jnp.where(channel == wanted, left[None], 0.0)
    spread_ref[...] = spread.reshape(PCH * (ROWS // POOL), R * PCH).astype(BF)
    for copy in shares:
        copy.wait_recv()
    @pl.when(has_left)
    def _():
        to_left.wait_send()

    @pl.when(has_right)
    def _():
        to_right.wait_send()

    for copy in inner + [inner_near] + outer + passes + shares:
        copy.wait_send()


def finale(track_ref, spread_ref, rights_ref, track_out, pair_ref, sem):
    copy = pltpu.make_async_copy(track_ref, track_out, sem)
    copy.start()
    every = jnp.concatenate([rights_ref[i].astype(F32) for i in range(GROUP)], axis=0).astype(BF)
    product = lax.dot_general(
        spread_ref[...], every, (((1,), (1,)), ((), ())), preferred_element_type=F32
    )
    pair_ref[...] = (
        (product * (1.0 / math.sqrt(R))).reshape(PCH, ROWS // POOL, GROUP * ROWS // POOL)
    ).astype(BF)
    copy.wait()


def body(x, conv_gain, conv_kernel, dilation, attn_gain, w_qkv, w_out, w_pair_a, w_pair_b):
    vmem = pl.BlockSpec(memory_space=pltpu.VMEM)
    hbm = pl.BlockSpec(memory_space=pl.ANY)
    track, spread, rights = pl.pallas_call(
        kernel,
        out_shape=(
            pltpu.VMEM((ROWS, C), BF),
            pltpu.VMEM((PCH * (ROWS // POOL), R * PCH), BF),
            pltpu.VMEM((GROUP, ROWS // POOL, R * PCH), BF),
        ),
        in_specs=[vmem, vmem, vmem, pl.BlockSpec(memory_space=pltpu.SMEM), vmem, hbm, hbm, hbm, hbm],
        out_specs=(vmem, vmem, vmem),
        scratch_shapes=[
            pltpu.VMEM(w_qkv.shape, BF),
            pltpu.VMEM(w_out.shape, BF),
            pltpu.VMEM(w_pair_a.shape, BF),
            pltpu.VMEM(w_pair_b.shape, BF),
            pltpu.VMEM((LAYERS, KSIZE, C), F32),
            pltpu.VMEM((CT, ROWS, LANES), F32),
            pltpu.VMEM((CT, SEG, 8, LANES), F32),
            pltpu.VMEM((CT, SEG + 2 * REACH, 8, LANES), F32),
            pltpu.VMEM((CT, ROWS, LANES), F32),
            pltpu.VMEM((2, EDGE, C), BF),
            pltpu.VMEM((2, ROWS, C), BF),
            pltpu.VMEM((2, ROWS, C), BF),
            pltpu.VMEM((GROUP * ROWS, C), BF),
            pltpu.VMEM((PAIRS, GROUP * ROWS, WIN), BF),
            pltpu.VMEM((PAIRS, 2 * ROWS, WIN), BF),
            pltpu.VMEM((PAIRS, 2 * ROWS, LANES), F32),
            pltpu.VMEM((PAIRS, 2 * ROWS, WIN), F32),
            pltpu.VMEM((ROWS, C), BF),
            pltpu.SemaphoreType.DMA((4,)),
            pltpu.SemaphoreType.DMA((16,)),
            pltpu.SemaphoreType.DMA((16,)),
        ],
        compiler_params=pltpu.CompilerParams(
            collective_id=0, has_side_effects=True, vmem_limit_bytes=60 * 1024 * 1024
        ),
    )(x, conv_gain, conv_kernel.transpose(1, 0, 2), dilation, attn_gain, w_qkv, w_out, w_pair_a, w_pair_b)
    return pl.pallas_call(
        finale,
        out_shape=(
            jax.ShapeDtypeStruct((ROWS, C), BF),
            jax.ShapeDtypeStruct((PCH, ROWS // POOL, GROUP * ROWS // POOL), BF),
        ),
        in_specs=[vmem, vmem, vmem],
        out_specs=(hbm, vmem),
        scratch_shapes=[pltpu.SemaphoreType.DMA],
        compiler_params=pltpu.CompilerParams(vmem_limit_bytes=32 * 1024 * 1024),
    )(*[pltpu.with_memory_space_constraint(v, pltpu.VMEM) for v in (track, spread, rights)])


def solution(mesh):
    placed = (P(("batch", "seq"), None), P(), P(), P(), P(), P(), P(), P(), P())
    return jax.shard_map(
        body,
        mesh=mesh,
        in_specs=placed,
        out_specs=(P(("batch", "seq"), None), P("batch", "seq", None)),
        check_vma=False,
    )
```
